32 devices in a mesh: groups: 2 (over y), shot: 8 (over z, x), slab: 2 (over core).
Axes of the slice: x: 2, y: 2, z: 4, core: 2. Of those that a mesh axis runs over, the one named last changes fastest.
Arguments:
- field_now: float32 [64, 8192], P('slab', ('groups', 'shot')), parts along dimension 1, may hold values from -6 to 6
- field_before: float32 [64, 8192], P('slab', ('groups', 'shot')), parts along dimension 1, may hold values from -6 to 6
- velocity: bfloat16 [64, 2048], P('slab', ('groups', 'shot')), parts along dimension 1, may hold values from 5 to 5.4375
- offsets: int32 [16], P(('groups', 'shot')), parts along dimension 0, may hold values from 0 to 512
- source_cell: int32 [16], P(('groups', 'shot')), parts along dimension 0, may hold values from 0 to 32767
- traces: bfloat16 [2, 4096, 256], P('slab', ('groups', 'shot')), parts along dimension 1, may hold values from -6 to 6
- trace_shot: int32 [2, 4096, 1], P('slab', ('groups', 'shot')), parts along dimension 1, may hold values from 0 to 7; in each aligned block of 256 rows (0 to 255, 256 to 511, ..., all dimensions but the last counted through in order) at most 64 rows name the same one
- trace_node_cell: int32 [2, 4096], P('slab', ('groups', 'shot')), parts along dimension 1, may hold values from 0 to 16383
Outputs:
- pressure: float32 [64, 8192], P('slab', ('groups', 'shot')), parts along dimension 1
The draws below stay inside these ranges and needn't reach their ends.
There are 2 independent parts, one for each index of `groups`. The reference program is written for one: setup_inputs(seed, part) draws one part's arguments, and reference() takes and returns one part's arrays. A program takes and returns all parts, laid end to end along the dimension named above; each array names one. Nothing has to cross between parts.
Inputs may be any that keep to these rules, and one draw needn't show every extreme that they name: `trace_shot`: among the trace rows of one device (aligned blocks of 256 rows along the second dimension, for each slab) at most 64 belong to one shot, and in some block some shot has exactly 64.
All inputs are finite; a program needn't handle non-finite values.
Results may differ from the reference program's by a relative error of at most 0.0003.
Values may be sent and summed in bfloat16 or wider, within the bound.
A program may use at most 64 MiB of HBM per device.

```python
import math
import jax
import jax.numpy as jnp
import numpy as np
from jax import lax

NS = 256
STEPS = 24
CZ = 32
W = 512
TR_DEV = 256
CAP = 64
NZ = 64
LX = 1024
N_SHOT = 8
N_SLAB = 2


def place_ends(array, stream_key, least, largest):
    longest = array.shape.index(max(array.shape))
    spots = []
    for shift in (0, 1):
        where = [jax.random.randint(jax.random.fold_in(stream_key, axis), (), 0, length) for axis, length in enumerate(array.shape)]
        where[longest] = (where[longest] + shift) % array.shape[longest]
        spots.append(tuple(where))
    return array.at[spots[0]].set(least).at[spots[1]].set(largest)


def shard_levels(rng, shape, shards, low, top_value):
    def one(axis_at, shards_of):
        heights = jax.random.uniform(jax.random.fold_in(jax.random.fold_in(rng, 6), axis_at), (shards_of,), jnp.float32, low / len(shards), top_value / len(shards))
        return jnp.repeat(jnp.exp(heights), shape[axis_at] // shards_of).reshape((-1,) + (1,) * (len(shape) - axis_at - 1))

    level = one(*shards[0])
    for cut in shards[1:]:
        level = level * one(*cut)
    return level


def shared_out(rng, own, number, rows, amount, top, bound, skew):
    sequence = jax.random.permutation(rng, amount)
    crowded, usual = shares(amount, rows * top, bound, skew, True), shares(amount, rows * top, bound, skew, False)
    places = jnp.arange(amount)

    def named(tallies, turn):
        used = int((tallies > 0).sum())
        fixed = max(1, used // 4)
        shifted = fixed + (places - fixed + turn * (used - fixed)) % max(1, amount - fixed)
        return jnp.zeros((amount,), jnp.int32).at[sequence[jnp.where(places < fixed, places, shifted)]].set(jnp.asarray(tallies, jnp.int32))

    tallies = jnp.where(number % 4 == 0, named(crowded, number // 4), named(usual, number - number // 4 - 1))
    mixed = jax.random.permutation(jax.random.fold_in(own, 3), amount)
    donor, receiver = mixed[0:amount // 2 * 2:2], mixed[1:amount // 2 * 2:2]
    room = jnp.minimum(tallies[donor] - 1, bound - tallies[receiver]) // 2
    room = jnp.where((donor == sequence[0]) | (receiver == sequence[0]) | (tallies[receiver] == 0), 0, jnp.maximum(room, 0))
    shifted = jax.random.randint(jax.random.fold_in(own, 4), (amount // 2,), 0, 1 << 20) % (room + 1)
    tallies = tallies.at[donor].add(-shifted).at[receiver].add(shifted)
    labels = jnp.searchsorted(jnp.cumsum(tallies), jnp.arange(rows * top), side="right").astype(jnp.int32)
    table = labels.reshape(top, rows).T
    table = table[jax.random.permutation(jax.random.fold_in(own, 1), rows)]
    turn = jax.random.randint(jax.random.fold_in(own, 2), (rows, 1), 0, top)
    return jnp.take_along_axis(table, (jnp.arange(top)[None, :] + turn) % top, axis=1)


def shares(amount, total, reach, skew, full):
    loads = [(1 << 20) // math.isqrt(rank ** skew) + 1 for rank in range(1, amount + 1)]
    largest = reach if full else min(reach, max(-(-total // amount), total * loads[0] // sum(loads)))
    least = 1 if total - largest >= amount - 1 else 0
    given, spare = [largest] + [least] * (amount - 1), total - largest - least * (amount - 1)
    while spare > 0:
        candidates = [i for i in range(1, amount) if given[i] < largest] or [i for i in range(1, amount) if given[i] < reach]
        whole, left = sum([loads[i] for i in candidates]), spare
        for i in candidates:
            addition = min(reach - given[i], max(1, left * loads[i] // whole), spare)
            given[i] = given[i] + addition
            spare = spare - addition
    return np.array(given)


def bell_draw(own_key, dims, deviation, limit, cuts=(), held_as=jnp.bfloat16):
    result = jax.random.normal(own_key, dims, jnp.float32) * deviation
    if len(cuts) > 0:
        result = shard_levels(own_key, dims, cuts, -0.22, 0.18) * result
    return jnp.clip(result, min=-limit, max=limit).astype(held_as)


def setup_inputs(seed: int = 0, part: int = 0) -> dict:
    keys = jax.random.split(jax.random.key(seed), 9)
    part_splits = jax.random.split(jax.random.fold_in(keys[8], part), 9)
    field_now = bell_draw(part_splits[0], (NZ, N_SHOT * W), 1.0, 6.0, ((0, 2), (1, 8)), jnp.float32)
    field_before = bell_draw(part_splits[1], (NZ, N_SHOT * W), 1.0, 6.0, ((0, 2), (1, 8)), jnp.float32)
    velocity = jnp.clip(5.0 + 0.4375 * jax.random.uniform(part_splits[2], (NZ, LX), jnp.float32) ** shard_levels(part_splits[2], (NZ, LX), ((0, 2), (1, 8)), -0.2, 0.2), 5.0, 5.4375).astype(jnp.bfloat16)
    offsets = place_ends(jax.random.randint(part_splits[3], (N_SHOT,), 0, LX - W + 1), jax.random.fold_in(part_splits[3], 1), 0, LX - W).astype(jnp.int32)
    source_cell = place_ends(jax.random.randint(part_splits[4], (N_SHOT,), 0, NZ * W), jax.random.fold_in(part_splits[4], 1), 0, (NZ * W) - 1).astype(jnp.int32)
    traces = bell_draw(part_splits[5], (N_SLAB, N_SHOT * TR_DEV, NS), 1.0, 6.0, ((0, 2), (1, 8)))
    trace_shot_keys = jax.random.split(jax.random.fold_in(part_splits[6], 1), N_SLAB * (N_SHOT * TR_DEV) // TR_DEV)
    trace_shot_turns = jax.random.permutation(jax.random.fold_in(part_splits[6], 3), N_SLAB * (N_SHOT * TR_DEV) // TR_DEV)
    trace_shot = jax.vmap(lambda own, number: shared_out(jax.random.fold_in(part_splits[6], 2), own, number, TR_DEV, N_SHOT, 1, CAP, 2))(trace_shot_keys, trace_shot_turns).reshape((N_SLAB, N_SHOT * TR_DEV, 1))
    trace_node_cell = place_ends(jax.random.randint(part_splits[7], (N_SLAB, N_SHOT * TR_DEV), 0, CZ * W), jax.random.fold_in(part_splits[7], 1), 0, (CZ * W) - 1).astype(jnp.int32)
    return dict(field_now=field_now, field_before=field_before, velocity=velocity, offsets=offsets, source_cell=source_cell, traces=traces, trace_shot=trace_shot, trace_node_cell=trace_node_cell)


LAP_CENTER = -205.0 / 72.0
LAP_TAPS = (1.6, -0.2, 8.0 / 315.0, -1.0 / 560.0)
PEAK = 0.12
DELAY = 5.0
SOURCE_GAIN = 2.0
RATIO = 0.1

def sample_table(sample_values, steps):
    kernel_step_index = jnp.arange(sample_values, dtype=jnp.float32)[:, None] + 0.5
    time_index = jnp.arange(steps, dtype=jnp.float32)[None, :] + 1.0
    return jnp.cos(math.pi * kernel_step_index * time_index / sample_values) * math.sqrt(2.0 / sample_values)

def ricker(step_value):
    argument = (math.pi * PEAK * (step_value - DELAY)) ** 2
    return (1.0 - 2.0 * argument) * jnp.exp(-argument)

def laplace(depth_padded, wavefield):
    depth_rows = wavefield.shape[-2]
    width_cols = wavefield.shape[-1]
    pads = [(0, 0)] * (wavefield.ndim - 1) + [(4, 4)]
    lateral_pad = jnp.pad(wavefield, pads)
    running_total = 2.0 * LAP_CENTER * wavefield
    for distance in range(1, 5):
        coeff = LAP_TAPS[distance - 1]
        running_total = running_total + coeff * (depth_padded[..., 4 + distance:4 + distance + depth_rows, :] + depth_padded[..., 4 - distance:4 - distance + depth_rows, :])
        running_total = running_total + coeff * (lateral_pad[..., 4 + distance:4 + distance + width_cols] + lateral_pad[..., 4 - distance:4 - distance + width_cols])
    return running_total

def reference(field_now, field_before, velocity, offsets, source_cell, traces, trace_shot, trace_node_cell):
    shots = offsets.shape[0]
    current = field_now.reshape(NZ, shots, W).transpose(1, 0, 2)
    previous = field_before.reshape(NZ, shots, W).transpose(1, 0, 2)
    column_index = offsets[:, None].astype(jnp.int32) + jnp.arange(W, dtype=jnp.int32)[None, :]
    window = jnp.take(velocity, column_index.reshape(-1), axis=1).reshape(NZ, shots, W).transpose(1, 0, 2)
    courant = jnp.square(window.astype(jnp.float32) * RATIO)
    table = sample_table(NS, STEPS)
    amplitude = jnp.dot(traces.reshape(-1, NS).astype(jnp.float32), table, precision=lax.Precision.HIGHEST)
    target = trace_shot.reshape(N_SLAB, -1).astype(jnp.int32)
    slabs = jnp.arange(N_SLAB, dtype=jnp.int32)[:, None]
    depth = slabs * CZ + trace_node_cell // W
    lateral = trace_node_cell % W
    flat_index = (target * (NZ * W) + depth * W + lateral).reshape(-1)
    cells = jnp.arange(NZ * W, dtype=jnp.int32)[None, :]
    source_mask = (cells == source_cell[:, None]).astype(jnp.float32).reshape(shots, NZ, W)

    def advance(step, carry):
        present, earlier = carry
        column = lax.dynamic_slice_in_dim(amplitude, step, 1, 1)[:, 0]
        injection = jnp.zeros((shots * NZ * W,), jnp.float32).at[flat_index].add(column).reshape(shots, NZ, W)
        injection = injection + SOURCE_GAIN * ricker(step.astype(jnp.float32)) * source_mask
        depth_padded = jnp.pad(present, ((0, 0), (4, 4), (0, 0)))
        advanced = 2.0 * present - earlier + courant * laplace(depth_padded, present) + injection
        return (advanced, present)
    current, previous = lax.fori_loop(0, STEPS, advance, (current, previous))
    return current.transpose(1, 0, 2).reshape(NZ, shots * W)
```

```python
import math

import jax
import jax.numpy as jnp
import numpy as np
from jax import lax
from jax.experimental import pallas as pl
from jax.experimental.pallas import tpu as pltpu
from jax.sharding import PartitionSpec as P

NS = 256
STEPS = 24
CAP = 64
LANES = 128
SUB = 8
ROWS = 32

LAP_CENTER = -205.0 / 72.0
LAP_TAPS = (1.6, -0.2, 8.0 / 315.0, -1.0 / 560.0)
PEAK = 0.12
DELAY = 5.0
SOURCE_GAIN = 2.0
RATIO = 0.1
NT = (((1,), (1,)), ((), ()))


def dot_nt(a, b):
    return lax.dot_general(a, b, NT, preferred_element_type=jnp.float32)


def split_table():
    k = np.arange(NS, dtype=np.float64)[:, None] + 0.5
    t = np.arange(STEPS, dtype=np.float64)[None, :] + 1.0
    table = np.cos(math.pi * k * t / NS) * math.sqrt(2.0 / NS)
    rest = np.zeros((ROWS, NS), np.float32)
    rest[:STEPS] = table.T
    parts = []
    for _ in range(3):
        part = rest.astype(jnp.bfloat16)
        parts.append(part)
        rest = rest - part.astype(np.float32)
    return jnp.asarray(np.concatenate(parts, axis=0))


def ricker_value(step):
    a = (math.pi * PEAK * (step - DELAY)) ** 2
    return SOURCE_GAIN * (1.0 - 2.0 * a) * math.exp(-a)


def exchange_kernel(
    shots, slabs, table_ref, now_ref, before_ref, velocity_ref, traces_ref, shot_ref, node_ref,
    gathered, fields, message, own, send_sem, recv_sem, field_send, field_recv,
):
    peers = shots * slabs
    shot, slab = lax.axis_index("shot"), lax.axis_index("slab")
    me = shot * slabs + slab
    depth, width = now_ref.shape
    groups = depth // SUB
    rows = traces_ref.shape[0]

    def place(d):
        index = lax.rem(me + d, peers)
        return index // slabs, lax.rem(index, slabs)

    barrier = pltpu.get_barrier_semaphore()

    def greet(d, carry):
        to_shot, to_slab = place(d)
        pl.semaphore_signal(
            barrier, inc=1, device_id={"shot": to_shot, "slab": to_slab},
            device_id_type=pl.DeviceIdType.MESH,
        )
        return carry

    lax.fori_loop(1, peers, greet, 0)

    for r in range(depth):
        to = (r % groups) * SUB + r // groups
        own[0, to : to + 1, :] = now_ref[r : r + 1, :]
        own[1, to : to + 1, :] = before_ref[r : r + 1, :]

    parts = dot_nt(table_ref[...], traces_ref[...])
    amplitude = parts[0:ROWS] + parts[ROWS : 2 * ROWS] + parts[2 * ROWS : 3 * ROWS]
    node = node_ref[...]
    lateral = node % width
    row = lax.broadcasted_iota(jnp.int32, (ROWS, rows), 0)
    where_to = jnp.where(
        row == STEPS, node // width, jnp.where(row == STEPS + 1, lateral // 256, lateral % 256)
    ).astype(jnp.float32)
    high = jnp.where(row < STEPS, amplitude, where_to).astype(jnp.bfloat16)
    low = jnp.where(row < STEPS, amplitude - high.astype(jnp.float32), where_to).astype(
        jnp.bfloat16
    )
    target = shot_ref[...]
    chosen = lax.broadcasted_iota(jnp.int32, (shots, rows), 0) == target
    onehot = jnp.where(chosen, 1.0, 0.0)
    ahead = jnp.where(
        lax.broadcasted_iota(jnp.int32, (rows, rows), 0)
        < lax.broadcasted_iota(jnp.int32, (rows, rows), 1),
        1.0, 0.0,
    ).astype(jnp.bfloat16)
    count = jnp.dot(onehot.astype(jnp.bfloat16), ahead, preferred_element_type=jnp.float32)
    position = jnp.sum(onehot * count, axis=0, keepdims=True)
    slot = lax.broadcasted_iota(jnp.int32, (LANES, rows), 0).astype(jnp.float32)

    turn = lax.broadcasted_iota(jnp.int32, (depth, depth), 0)
    turned = jnp.where(
        (turn % SUB) * groups + turn // SUB
        == lax.broadcasted_iota(jnp.int32, (depth, depth), 1),
        1.0, 0.0,
    ).astype(jnp.bfloat16)
    panel = jnp.dot(turned, velocity_ref[...], preferred_element_type=jnp.float32).astype(
        jnp.bfloat16
    )

    def fill(s, carry):
        mine = target == s
        to_high = jnp.where(mine, position, -1.0)
        to_low = jnp.where(mine, position + float(CAP), -1.0)
        pick_high = jnp.where(slot == to_high, 1.0, 0.0).astype(jnp.bfloat16)
        pick_low = jnp.where(slot == to_low, 1.0, 0.0).astype(jnp.bfloat16)
        message[s, 0] = (dot_nt(high, pick_high) + dot_nt(low, pick_low)).astype(jnp.bfloat16)
        message[s, 1] = panel
        return carry

    lax.fori_loop(0, shots, fill, 0, unroll=shots <= 8)

    pl.semaphore_wait(barrier, peers - 1)

    def field_copy(d):
        return pltpu.make_async_remote_copy(
            src_ref=own, dst_ref=fields.at[slab],
            send_sem=field_send.at[d], recv_sem=field_recv.at[d],
            device_id={"slab": lax.rem(slab + d, slabs)},
            device_id_type=pl.DeviceIdType.MESH,
        )

    def message_copy(d):
        to_shot, to_slab = place(d)
        return pltpu.make_async_remote_copy(
            src_ref=message.at[to_shot], dst_ref=gathered.at[slab, shot],
            send_sem=send_sem.at[d], recv_sem=recv_sem.at[d],
            device_id={"shot": to_shot, "slab": to_slab},
            device_id_type=pl.DeviceIdType.MESH,
        )

    def start_message(d, carry):
        message_copy(d).start()
        return carry

    def start_field(d, carry):
        field_copy(d).start()
        return carry

    def wait_message(d, carry):
        message_copy(d).wait()
        return carry

    def wait_field(d, carry):
        field_copy(d).wait()
        return carry

    lax.fori_loop(1, peers, start_message, 0)
    lax.fori_loop(1, slabs, start_field, 0)
    gathered[slab, shot] = message[shot]
    fields[slab] = own[...]
    lax.fori_loop(1, slabs, wait_field, 0)
    lax.fori_loop(1, peers, wait_message, 0)


def wave_kernel(
    shots, slabs, offset_ref, source_ref, gathered, fields, out_ref,
    injection, left, right, courant, first, second,
):
    depth, width = out_ref.shape
    groups = depth // SUB
    columns = width // LANES
    slab = lax.axis_index("slab")
    few = slabs <= 2

    lane = lax.broadcasted_iota(jnp.int32, (SUB, LANES), 1)
    sub = lax.broadcasted_iota(jnp.int32, (SUB, LANES), 0)
    offset = offset_ref[0]
    panel0 = offset // LANES
    shift = offset % LANES
    keep = lax.broadcasted_iota(jnp.int32, (depth, LANES), 1) < LANES - shift
    at_row = lax.broadcasted_iota(jnp.int32, (depth, LANES), 0)
    row_depth = ((at_row % SUB) * groups + at_row // SUB).astype(jnp.float32)
    at_cell = lax.broadcasted_iota(jnp.int32, (width, LANES), 0).astype(jnp.float32)

    def prepare(j, carry):
        turned = []
        for c in range(columns + 1):
            panel = jnp.minimum(panel0 + c, shots - 1)
            turned.append(
                pltpu.roll(
                    gathered[j, panel, 1].astype(jnp.float32), lax.rem(LANES - shift, LANES), 1
                )
            )
        for c in range(columns):
            window = jnp.where(keep, turned[c], turned[c + 1]) * RATIO
            courant[j, :, c * LANES : (c + 1) * LANES] = window * window

        def source(s, inner):
            lanes = pl.ds(pl.multiple_of(s * LANES, LANES), LANES)
            values = gathered[j, s, 0].astype(jnp.float32)
            at_depth = values[STEPS : STEPS + 1]
            at_lateral = values[STEPS + 1 : STEPS + 2] * 256.0 + values[STEPS + 2 : STEPS + 3]
            chosen = row_depth == at_depth
            for t in range(STEPS):
                left[t * depth : (t + 1) * depth, lanes] = jnp.where(
                    chosen, values[t : t + 1], 0.0
                ).astype(jnp.bfloat16)
            right[:, lanes] = jnp.where(at_cell == at_lateral, 1.0, 0.0).astype(jnp.bfloat16)
            return inner

        lax.fori_loop(0, shots, source, 0, unroll=shots <= 8)
        injection[j] = dot_nt(left[...], right[...])
        first[j] = fields[j, 0]
        second[j] = fields[j, 1]
        return carry

    lax.fori_loop(0, slabs, prepare, 0, unroll=few)

    source = source_ref[0]
    source_depth = source // width
    source_slab = source_depth // depth
    within = source_depth % depth
    source_row = (within % groups) * SUB + within // groups
    here = lax.broadcasted_iota(jnp.int32, (1, width), 1) == source % width
    for t in range(STEPS):
        spot = pl.ds(t * depth + source_row, 1)
        injection[source_slab, spot, :] = injection[source_slab, spot, :] + jnp.where(
            here, ricker_value(float(t)), 0.0
        )

    def step(t, now, other):
        def one_slab(j, carry):
            def cell(jj, v, c):
                return now[jj, v * SUB : (v + 1) * SUB, c * LANES : (c + 1) * LANES]

            up_ok = jnp.where(j + 1 < slabs, 1.0, 0.0) if not few else None
            down_ok = jnp.where(j > 0, 1.0, 0.0) if not few else None

            def ups(v, c):
                base = pltpu.roll(cell(j, v, c), SUB - 1, 0)
                if few:
                    beyond = pltpu.roll(cell(j + 1, v, c), SUB - 1, 0) if j + 1 < slabs else 0.0
                else:
                    beyond = pltpu.roll(cell(jnp.minimum(j + 1, slabs - 1), v, c), SUB - 1, 0)
                    beyond = beyond * up_ok
                return jnp.where(sub == SUB - 1, beyond, base)

            def downs(v, c):
                base = pltpu.roll(cell(j, v, c), 1, 0)
                if few:
                    beyond = pltpu.roll(cell(j - 1, v, c), 1, 0) if j > 0 else 0.0
                else:
                    beyond = pltpu.roll(cell(jnp.maximum(j - 1, 0), v, c), 1, 0) * down_ok
                return jnp.where(sub == 0, beyond, base)

            up = [[ups(v, c) for c in range(columns)] for v in range(groups)]
            down = [[downs(v, c) for c in range(columns)] for v in range(groups)]
            for v in range(groups):
                line = [cell(j, v, c) for c in range(columns)]
                totals = [LAP_CENTER * 2.0 * line[c] for c in range(columns)]
                for k in range(1, 5):
                    plus = [pltpu.roll(line[c], LANES - k, 1) for c in range(columns)]
                    minus = [pltpu.roll(line[c], k, 1) for c in range(columns)]
                    for c in range(columns):
                        after = plus[c + 1] if c + 1 < columns else 0.0
                        prior = minus[c - 1] if c > 0 else 0.0
                        sides = jnp.where(lane < LANES - k, plus[c], after) + jnp.where(
                            lane < k, prior, minus[c]
                        )
                        below = cell(j, v + k, c) if v + k < groups else up[v + k - groups][c]
                        above = cell(j, v - k, c) if v >= k else down[v - k + groups][c]
                        totals[c] = totals[c] + LAP_TAPS[k - 1] * (sides + (below + above))
                for c in range(columns):
                    rows = slice(v * SUB, (v + 1) * SUB)
                    lanes = slice(c * LANES, (c + 1) * LANES)
                    start = pl.multiple_of(t * depth + v * SUB, SUB)
                    other[j, rows, lanes] = (
                        2.0 * line[c]
                        - other[j, rows, lanes]
                        + courant[j, rows, lanes] * totals[c]
                        + injection[j, pl.ds(start, SUB), lanes]
                    )
            return carry

        if few:
            for j in range(slabs):
                one_slab(j, 0)
        else:
            lax.fori_loop(0, slabs, one_slab, 0)

    def pair(i, carry):
        step(2 * i, first, second)
        step(2 * i + 1, second, first)
        return carry

    lax.fori_loop(0, STEPS // 2, pair, 0)
    for r in range(depth):
        at = (r % groups) * SUB + r // groups
        out_ref[r : r + 1, :] = first[slab, at : at + 1, :]


def local(
    field_now, field_before, velocity, offsets, source_cell, traces, trace_shot, trace_node_cell
):
    depth, width = field_now.shape
    shots, slabs = lax.axis_size("shot"), lax.axis_size("slab")
    rows = traces.shape[1]
    vmem = pl.BlockSpec(memory_space=pltpu.VMEM)
    smem = pl.BlockSpec(memory_space=pltpu.SMEM)
    def exchange(*refs):
        exchange_kernel(shots, slabs, *refs)

    def wave(*refs):
        wave_kernel(shots, slabs, *refs)

    gathered, fields = pl.pallas_call(
        exchange,
        out_shape=(
            jax.ShapeDtypeStruct((slabs, shots, 2, depth, LANES), jnp.bfloat16),
            jax.ShapeDtypeStruct((slabs, 2, depth, width), jnp.float32),
        ),
        in_specs=[vmem] * 7,
        out_specs=(vmem, vmem),
        scratch_shapes=[
            pltpu.VMEM((shots, 2, depth, LANES), jnp.bfloat16),
            pltpu.VMEM((2, depth, width), jnp.float32),
            pltpu.SemaphoreType.DMA((shots * slabs,)),
            pltpu.SemaphoreType.DMA((shots * slabs,)),
            pltpu.SemaphoreType.DMA((slabs,)),
            pltpu.SemaphoreType.DMA((slabs,)),
        ],
        compiler_params=pltpu.CompilerParams(
            collective_id=0, has_side_effects=True, vmem_limit_bytes=48 << 20
        ),
    )(
        split_table(), field_now, field_before, velocity, traces[0],
        trace_shot.reshape(1, rows), trace_node_cell,
    )
    return pl.pallas_call(
        wave,
        out_shape=jax.ShapeDtypeStruct((depth, width), jnp.float32),
        in_specs=[smem, smem, vmem, vmem],
        out_specs=vmem,
        scratch_shapes=[
            pltpu.VMEM((slabs, STEPS * depth, width), jnp.float32),
            pltpu.VMEM((STEPS * depth, shots * LANES), jnp.bfloat16),
            pltpu.VMEM((width, shots * LANES), jnp.bfloat16),
            pltpu.VMEM((slabs, depth, width), jnp.float32),
            pltpu.VMEM((slabs, depth, width), jnp.float32),
            pltpu.VMEM((slabs, depth, width), jnp.float32),
        ],
        compiler_params=pltpu.CompilerParams(vmem_limit_bytes=48 << 20),
    )(offsets, source_cell, gathered, fields)


def solution(mesh):
    in_specs = (
        P("slab", ("groups", "shot")),
        P("slab", ("groups", "shot")),
        P("slab", ("groups", "shot")),
        P(("groups", "shot")),
        P(("groups", "shot")),
        P("slab", ("groups", "shot"), None),
        P("slab", ("groups", "shot"), None),
        P("slab", ("groups", "shot")),
    )
    out_specs = P("slab", ("groups", "shot"))
    return jax.shard_map(local, mesh=mesh, in_specs=in_specs, out_specs=out_specs, check_vma=False)
```

```python
import math

import jax
import jax.numpy as jnp
import numpy as np
from jax import lax
from jax.experimental import pallas as pl
from jax.experimental.pallas import tpu as pltpu
from jax.sharding import PartitionSpec as P

NS = 256
STEPS = 24
CAP = 64
LANES = 128
SUB = 8
ROWS = 32

LAP_CENTER = -205.0 / 72.0
LAP_TAPS = (1.6, -0.2, 8.0 / 315.0, -1.0 / 560.0)
PEAK = 0.12
DELAY = 5.0
SOURCE_GAIN = 2.0
RATIO = 0.1
NT = (((1,), (1,)), ((), ()))


def dot_nt(a, b):
    return lax.dot_general(a, b, NT, preferred_element_type=jnp.float32)


def split_table():
    k = np.arange(NS, dtype=np.float64)[:, None] + 0.5
    t = np.arange(STEPS, dtype=np.float64)[None, :] + 1.0
    table = np.cos(math.pi * k * t / NS) * math.sqrt(2.0 / NS)
    rest = np.zeros((ROWS, NS), np.float32)
    rest[:STEPS] = table.T
    parts = []
    for _ in range(3):
        part = rest.astype(jnp.bfloat16)
        parts.append(part)
        rest = rest - part.astype(np.float32)
    return jnp.asarray(np.concatenate(parts, axis=0))


def ricker_value(step):
    a = (math.pi * PEAK * (step - DELAY)) ** 2
    return SOURCE_GAIN * (1.0 - 2.0 * a) * math.exp(-a)


def exchange_kernel(
    shots, slabs, table_hbm, now_hbm, before_hbm, velocity_hbm, traces_hbm, shot_hbm, node_hbm,
    gathered, fields, message, own, send_sem, recv_sem, field_send, field_recv,
    table_ref, now_ref, before_ref, velocity_ref, traces_ref, shot_ref, node_ref, load_sem,
):
    peers = shots * slabs
    shot, slab = lax.axis_index("shot"), lax.axis_index("slab")
    me = shot * slabs + slab
    depth, width = now_ref.shape
    groups = depth // SUB
    rows = traces_ref.shape[0]

    loads = [
        pltpu.make_async_copy(source, to, load_sem.at[i])
        for i, (source, to) in enumerate(
            (
                (traces_hbm, traces_ref), (shot_hbm, shot_ref), (node_hbm, node_ref),
                (table_hbm, table_ref), (velocity_hbm, velocity_ref),
                (now_hbm, now_ref), (before_hbm, before_ref),
            )
        )
    ]
    for load in loads:
        load.start()

    def place(d):
        index = lax.rem(me + d, peers)
        return index // slabs, lax.rem(index, slabs)

    barrier = pltpu.get_barrier_semaphore()

    def greet(d, carry):
        to_shot, to_slab = place(d)
        pl.semaphore_signal(
            barrier, inc=1, device_id={"shot": to_shot, "slab": to_slab},
            device_id_type=pl.DeviceIdType.MESH,
        )
        return carry

    lax.fori_loop(1, peers, greet, 0)

    for load in loads[:5]:
        load.wait()
    parts = dot_nt(table_ref[...], traces_ref[...])
    amplitude = parts[0:ROWS] + parts[ROWS : 2 * ROWS] + parts[2 * ROWS : 3 * ROWS]
    node = node_ref[...]
    lateral = node % width
    row = lax.broadcasted_iota(jnp.int32, (ROWS, rows), 0)
    where_to = jnp.where(
        row == STEPS, node // width, jnp.where(row == STEPS + 1, lateral // 256, lateral % 256)
    ).astype(jnp.float32)
    high = jnp.where(row < STEPS, amplitude, where_to).astype(jnp.bfloat16)
    low = jnp.where(row < STEPS, amplitude - high.astype(jnp.float32), where_to).astype(
        jnp.bfloat16
    )
    target = shot_ref[...]
    chosen = lax.broadcasted_iota(jnp.int32, (shots, rows), 0) == target
    onehot = jnp.where(chosen, 1.0, 0.0)
    ahead = jnp.where(
        lax.broadcasted_iota(jnp.int32, (rows, rows), 0)
        < lax.broadcasted_iota(jnp.int32, (rows, rows), 1),
        1.0, 0.0,
    ).astype(jnp.bfloat16)
    count = jnp.dot(onehot.astype(jnp.bfloat16), ahead, preferred_element_type=jnp.float32)
    position = jnp.sum(onehot * count, axis=0, keepdims=True)
    slot = lax.broadcasted_iota(jnp.int32, (LANES, rows), 0).astype(jnp.float32)

    turn = lax.broadcasted_iota(jnp.int32, (depth, depth), 0)
    turned = jnp.where(
        (turn % SUB) * groups + turn // SUB
        == lax.broadcasted_iota(jnp.int32, (depth, depth), 1),
        1.0, 0.0,
    ).astype(jnp.bfloat16)
    panel = jnp.dot(turned, velocity_ref[...], preferred_element_type=jnp.float32).astype(
        jnp.bfloat16
    )

    def fill(s, carry):
        mine = target == s
        to_high = jnp.where(mine, position, -1.0)
        to_low = jnp.where(mine, position + float(CAP), -1.0)
        pick_high = jnp.where(slot == to_high, 1.0, 0.0).astype(jnp.bfloat16)
        pick_low = jnp.where(slot == to_low, 1.0, 0.0).astype(jnp.bfloat16)
        message[s, 0] = (dot_nt(high, pick_high) + dot_nt(low, pick_low)).astype(jnp.bfloat16)
        message[s, 1] = panel
        return carry

    lax.fori_loop(0, shots, fill, 0, unroll=shots <= 8)

    for load in loads[5:]:
        load.wait()
    for r in range(depth):
        to = (r % groups) * SUB + r // groups
        own[0, to : to + 1, :] = now_ref[r : r + 1, :]
        own[1, to : to + 1, :] = before_ref[r : r + 1, :]
    pl.semaphore_wait(barrier, peers - 1)

    def field_copy(d):
        return pltpu.make_async_remote_copy(
            src_ref=own, dst_ref=fields.at[slab],
            send_sem=field_send.at[d], recv_sem=field_recv.at[d],
            device_id={"slab": lax.rem(slab + d, slabs)},
            device_id_type=pl.DeviceIdType.MESH,
        )

    def message_copy(d):
        to_shot, to_slab = place(d)
        return pltpu.make_async_remote_copy(
            src_ref=message.at[to_shot], dst_ref=gathered.at[slab, shot],
            send_sem=send_sem.at[d], recv_sem=recv_sem.at[d],
            device_id={"shot": to_shot, "slab": to_slab},
            device_id_type=pl.DeviceIdType.MESH,
        )

    def start_message(d, carry):
        message_copy(d).start()
        return carry

    def start_field(d, carry):
        field_copy(d).start()
        return carry

    def wait_message(d, carry):
        message_copy(d).wait()
        return carry

    def wait_field(d, carry):
        field_copy(d).wait()
        return carry

    lax.fori_loop(1, slabs, start_field, 0)
    lax.fori_loop(1, peers, start_message, 0)
    keep_message = pltpu.make_async_copy(
        message.at[shot], gathered.at[slab, shot], load_sem.at[0]
    )
    keep_field = pltpu.make_async_copy(own, fields.at[slab], load_sem.at[1])
    keep_message.start()
    keep_field.start()
    lax.fori_loop(1, slabs, wait_field, 0)
    lax.fori_loop(1, peers, wait_message, 0)
    keep_message.wait()
    keep_field.wait()


def wave_kernel(
    shots, slabs, offset_ref, source_ref, gathered_hbm, fields_hbm, out_ref,
    injection, left, right, courant, first, second, gathered, load_sem,
):
    depth, width = out_ref.shape
    groups = depth // SUB
    columns = width // LANES
    slab = lax.axis_index("slab")
    few = slabs <= 2

    load_gathered = pltpu.make_async_copy(gathered_hbm, gathered, load_sem.at[0])
    load_first = pltpu.make_async_copy(fields_hbm.at[:, 0], first, load_sem.at[1])
    load_second = pltpu.make_async_copy(fields_hbm.at[:, 1], second, load_sem.at[2])
    load_gathered.start()
    load_first.start()
    load_second.start()
    load_gathered.wait()
    lane = lax.broadcasted_iota(jnp.int32, (SUB, LANES), 1)
    sub = lax.broadcasted_iota(jnp.int32, (SUB, LANES), 0)
    offset = offset_ref[0]
    panel0 = offset // LANES
    shift = offset % LANES
    keep = lax.broadcasted_iota(jnp.int32, (depth, LANES), 1) < LANES - shift
    at_row = lax.broadcasted_iota(jnp.int32, (depth, LANES), 0)
    row_depth = ((at_row % SUB) * groups + at_row // SUB).astype(jnp.float32)
    at_cell = lax.broadcasted_iota(jnp.int32, (width, LANES), 0).astype(jnp.float32)

    def prepare(j, carry):
        turned = []
        for c in range(columns + 1):
            panel = jnp.minimum(panel0 + c, shots - 1)
            turned.append(
                pltpu.roll(
                    gathered[j, panel, 1].astype(jnp.float32), lax.rem(LANES - shift, LANES), 1
                )
            )
        for c in range(columns):
            window = jnp.where(keep, turned[c], turned[c + 1]) * RATIO
            courant[j, :, c * LANES : (c + 1) * LANES] = window * window

        def source(s, inner):
            lanes = pl.ds(pl.multiple_of(s * LANES, LANES), LANES)
            values = gathered[j, s, 0].astype(jnp.float32)
            at_depth = values[STEPS : STEPS + 1]
            at_lateral = values[STEPS + 1 : STEPS + 2] * 256.0 + values[STEPS + 2 : STEPS + 3]
            chosen = row_depth == at_depth
            for t in range(STEPS):
                left[t * depth : (t + 1) * depth, lanes] = jnp.where(
                    chosen, values[t : t + 1], 0.0
                ).astype(jnp.bfloat16)
            right[:, lanes] = jnp.where(at_cell == at_lateral, 1.0, 0.0).astype(jnp.bfloat16)
            return inner

        lax.fori_loop(0, shots, source, 0, unroll=shots <= 8)
        injection[j] = dot_nt(left[...], right[...])
        return carry

    lax.fori_loop(0, slabs, prepare, 0, unroll=few)

    source = source_ref[0]
    source_depth = source // width
    source_slab = source_depth // depth
    within = source_depth % depth
    source_row = (within % groups) * SUB + within // groups
    here = lax.broadcasted_iota(jnp.int32, (1, width), 1) == source % width
    for t in range(STEPS):
        spot = pl.ds(t * depth + source_row, 1)
        injection[source_slab, spot, :] = injection[source_slab, spot, :] + jnp.where(
            here, ricker_value(float(t)), 0.0
        )

    load_first.wait()
    load_second.wait()

    def step(t, now, other):
        def one_slab(j, carry):
            def cell(jj, v, c):
                return now[jj, v * SUB : (v + 1) * SUB, c * LANES : (c + 1) * LANES]

            up_ok = jnp.where(j + 1 < slabs, 1.0, 0.0) if not few else None
            down_ok = jnp.where(j > 0, 1.0, 0.0) if not few else None

            def ups(v, c):
                base = pltpu.roll(cell(j, v, c), SUB - 1, 0)
                if few:
                    beyond = pltpu.roll(cell(j + 1, v, c), SUB - 1, 0) if j + 1 < slabs else 0.0
                else:
                    beyond = pltpu.roll(cell(jnp.minimum(j + 1, slabs - 1), v, c), SUB - 1, 0)
                    beyond = beyond * up_ok
                return jnp.where(sub == SUB - 1, beyond, base)

            def downs(v, c):
                base = pltpu.roll(cell(j, v, c), 1, 0)
                if few:
                    beyond = pltpu.roll(cell(j - 1, v, c), 1, 0) if j > 0 else 0.0
                else:
                    beyond = pltpu.roll(cell(jnp.maximum(j - 1, 0), v, c), 1, 0) * down_ok
                return jnp.where(sub == 0, beyond, base)

            up = [[ups(v, c) for c in range(columns)] for v in range(groups)]
            down = [[downs(v, c) for c in range(columns)] for v in range(groups)]
            for v in range(groups):
                line = [cell(j, v, c) for c in range(columns)]
                totals = [LAP_CENTER * 2.0 * line[c] for c in range(columns)]
                for k in range(1, 5):
                    plus = [pltpu.roll(line[c], LANES - k, 1) for c in range(columns)]
                    minus = [pltpu.roll(line[c], k, 1) for c in range(columns)]
                    for c in range(columns):
                        after = plus[c + 1] if c + 1 < columns else 0.0
                        prior = minus[c - 1] if c > 0 else 0.0
                        sides = jnp.where(lane < LANES - k, plus[c], after) + jnp.where(
                            lane < k, prior, minus[c]
                        )
                        below = cell(j, v + k, c) if v + k < groups else up[v + k - groups][c]
                        above = cell(j, v - k, c) if v >= k else down[v - k + groups][c]
                        totals[c] = totals[c] + LAP_TAPS[k - 1] * (sides + (below + above))
                for c in range(columns):
                    rows = slice(v * SUB, (v + 1) * SUB)
                    lanes = slice(c * LANES, (c + 1) * LANES)
                    start = pl.multiple_of(t * depth + v * SUB, SUB)
                    other[j, rows, lanes] = (
                        2.0 * line[c]
                        - other[j, rows, lanes]
                        + courant[j, rows, lanes] * totals[c]
                        + injection[j, pl.ds(start, SUB), lanes]
                    )
            return carry

        if few:
            for j in range(slabs):
                one_slab(j, 0)
        else:
            lax.fori_loop(0, slabs, one_slab, 0)

    def pair(i, carry):
        step(2 * i, first, second)
        step(2 * i + 1, second, first)
        return carry

    lax.fori_loop(0, STEPS // 2, pair, 0)
    for r in range(depth):
        at = (r % groups) * SUB + r // groups
        out_ref[r : r + 1, :] = first[slab, at : at + 1, :]


def local(
    field_now, field_before, velocity, offsets, source_cell, traces, trace_shot, trace_node_cell
):
    depth, width = field_now.shape
    shots, slabs = lax.axis_size("shot"), lax.axis_size("slab")
    rows = traces.shape[1]
    vmem = pl.BlockSpec(memory_space=pltpu.VMEM)
    hbm = pl.BlockSpec(memory_space=pltpu.HBM)
    smem = pl.BlockSpec(memory_space=pltpu.SMEM)
    def exchange(*refs):
        exchange_kernel(shots, slabs, *refs)

    def wave(*refs):
        wave_kernel(shots, slabs, *refs)

    gathered, fields = pl.pallas_call(
        exchange,
        out_shape=(
            jax.ShapeDtypeStruct((slabs, shots, 2, depth, LANES), jnp.bfloat16),
            jax.ShapeDtypeStruct((slabs, 2, depth, width), jnp.float32),
        ),
        in_specs=[hbm] * 7,
        out_specs=(hbm, hbm),
        scratch_shapes=[
            pltpu.VMEM((shots, 2, depth, LANES), jnp.bfloat16),
            pltpu.VMEM((2, depth, width), jnp.float32),
            pltpu.SemaphoreType.DMA((shots * slabs,)),
            pltpu.SemaphoreType.DMA((shots * slabs,)),
            pltpu.SemaphoreType.DMA((slabs,)),
            pltpu.SemaphoreType.DMA((slabs,)),
            pltpu.VMEM((3 * ROWS, NS), jnp.bfloat16),
            pltpu.VMEM((depth, width), jnp.float32),
            pltpu.VMEM((depth, width), jnp.float32),
            pltpu.VMEM(velocity.shape, jnp.bfloat16),
            pltpu.VMEM((rows, NS), jnp.bfloat16),
            pltpu.VMEM((1, rows), jnp.int32),
            pltpu.VMEM((1, rows), jnp.int32),
            pltpu.SemaphoreType.DMA((7,)),
        ],
        compiler_params=pltpu.CompilerParams(
            collective_id=0, has_side_effects=True, vmem_limit_bytes=63 << 20
        ),
    )(
        split_table(), field_now, field_before, velocity, traces[0],
        trace_shot.reshape(1, rows), trace_node_cell,
    )
    return pl.pallas_call(
        wave,
        out_shape=jax.ShapeDtypeStruct((depth, width), jnp.float32),
        in_specs=[smem, smem, hbm, hbm],
        out_specs=vmem,
        scratch_shapes=[
            pltpu.VMEM((slabs, STEPS * depth, width), jnp.float32),
            pltpu.VMEM((STEPS * depth, shots * LANES), jnp.bfloat16),
            pltpu.VMEM((width, shots * LANES), jnp.bfloat16),
            pltpu.VMEM((slabs, depth, width), jnp.float32),
            pltpu.VMEM((slabs, depth, width), jnp.float32),
            pltpu.VMEM((slabs, depth, width), jnp.float32),
            pltpu.VMEM((slabs, shots, 2, depth, LANES), jnp.bfloat16),
            pltpu.SemaphoreType.DMA((3,)),
        ],
        compiler_params=pltpu.CompilerParams(vmem_limit_bytes=63 << 20),
    )(offsets, source_cell, gathered, fields)


def solution(mesh):
    in_specs = (
        P("slab", ("groups", "shot")),
        P("slab", ("groups", "shot")),
        P("slab", ("groups", "shot")),
        P(("groups", "shot")),
        P(("groups", "shot")),
        P("slab", ("groups", "shot"), None),
        P("slab", ("groups", "shot"), None),
        P("slab", ("groups", "shot")),
    )
    out_specs = P("slab", ("groups", "shot"))
    return jax.shard_map(local, mesh=mesh, in_specs=in_specs, out_specs=out_specs, check_vma=False)
```

```python
import math

import jax
import jax.numpy as jnp
import numpy as np
from jax import lax
from jax.experimental import pallas as pl
from jax.experimental.pallas import tpu as pltpu
from jax.sharding import PartitionSpec as P

NS = 256
STEPS = 24
CAP = 64
LANES = 128
SUB = 8
ROWS = 32

LAP_CENTER = -205.0 / 72.0
LAP_TAPS = (1.6, -0.2, 8.0 / 315.0, -1.0 / 560.0)
PEAK = 0.12
DELAY = 5.0
SOURCE_GAIN = 2.0
RATIO = 0.1
NT = (((1,), (1,)), ((), ()))


def dot_nt(a, b):
    return lax.dot_general(a, b, NT, preferred_element_type=jnp.float32)


def split_table():
    k = np.arange(NS, dtype=np.float64)[:, None] + 0.5
    t = np.arange(STEPS, dtype=np.float64)[None, :] + 1.0
    table = np.cos(math.pi * k * t / NS) * math.sqrt(2.0 / NS)
    rest = np.zeros((ROWS, NS), np.float32)
    rest[:STEPS] = table.T
    parts = []
    for _ in range(3):
        part = rest.astype(jnp.bfloat16)
        parts.append(part)
        rest = rest - part.astype(np.float32)
    return jnp.asarray(np.concatenate(parts, axis=0))


def ricker_value(step):
    a = (math.pi * PEAK * (step - DELAY)) ** 2
    return SOURCE_GAIN * (1.0 - 2.0 * a) * math.exp(-a)


def exchange_kernel(
    shots, slabs, table_hbm, now_hbm, before_hbm, velocity_hbm, traces_hbm, shot_hbm, node_hbm,
    gathered, fields, message, own, send_sem, recv_sem, field_send, field_recv, relay_send, relay_recv,
    table_ref, now_ref, before_ref, velocity_ref, traces_ref, shot_ref, node_ref, load_sem,
):
    shot, slab = lax.axis_index("shot"), lax.axis_index("slab")
    depth, width = now_ref.shape
    groups = depth // SUB
    rows = traces_ref.shape[0]

    loads = [
        pltpu.make_async_copy(source, to, load_sem.at[i])
        for i, (source, to) in enumerate(
            (
                (traces_hbm, traces_ref), (shot_hbm, shot_ref), (node_hbm, node_ref),
                (table_hbm, table_ref), (velocity_hbm, velocity_ref),
                (now_hbm, now_ref), (before_hbm, before_ref),
            )
        )
    ]
    for load in loads:
        load.start()

    barrier = pltpu.get_barrier_semaphore()

    def greet_shot(d, carry):
        pl.semaphore_signal(
            barrier, inc=1, device_id={"shot": lax.rem(shot + d, shots)},
            device_id_type=pl.DeviceIdType.MESH,
        )
        return carry

    def greet_slab(d, carry):
        pl.semaphore_signal(
            barrier, inc=1, device_id={"slab": lax.rem(slab + d, slabs)},
            device_id_type=pl.DeviceIdType.MESH,
        )
        return carry

    lax.fori_loop(1, shots, greet_shot, 0)
    lax.fori_loop(1, slabs, greet_slab, 0)

    for load in loads[:5]:
        load.wait()
    parts = dot_nt(table_ref[...], traces_ref[...])
    amplitude = parts[0:ROWS] + parts[ROWS : 2 * ROWS] + parts[2 * ROWS : 3 * ROWS]
    node = node_ref[...]
    lateral = node % width
    row = lax.broadcasted_iota(jnp.int32, (ROWS, rows), 0)
    where_to = jnp.where(
        row == STEPS, node // width, jnp.where(row == STEPS + 1, lateral // 256, lateral % 256)
    ).astype(jnp.float32)
    high = jnp.where(row < STEPS, amplitude, where_to).astype(jnp.bfloat16)
    low = jnp.where(row < STEPS, amplitude - high.astype(jnp.float32), where_to).astype(
        jnp.bfloat16
    )
    target = shot_ref[...]
    chosen = lax.broadcasted_iota(jnp.int32, (shots, rows), 0) == target
    onehot = jnp.where(chosen, 1.0, 0.0)
    ahead = jnp.where(
        lax.broadcasted_iota(jnp.int32, (rows, rows), 0)
        < lax.broadcasted_iota(jnp.int32, (rows, rows), 1),
        1.0, 0.0,
    ).astype(jnp.bfloat16)
    count = jnp.dot(onehot.astype(jnp.bfloat16), ahead, preferred_element_type=jnp.float32)
    position = jnp.sum(onehot * count, axis=0, keepdims=True)
    slot = lax.broadcasted_iota(jnp.int32, (LANES, rows), 0).astype(jnp.float32)

    turn = lax.broadcasted_iota(jnp.int32, (depth, depth), 0)
    turned = jnp.where(
        (turn % SUB) * groups + turn // SUB
        == lax.broadcasted_iota(jnp.int32, (depth, depth), 1),
        1.0, 0.0,
    ).astype(jnp.bfloat16)
    panel = jnp.dot(turned, velocity_ref[...], preferred_element_type=jnp.float32).astype(
        jnp.bfloat16
    )

    def fill(d, carry):
        s = lax.rem(shot + d, shots)
        mine = target == s
        to_high = jnp.where(mine, position, -1.0)
        to_low = jnp.where(mine, position + float(CAP), -1.0)
        pick_high = jnp.where(slot == to_high, 1.0, 0.0).astype(jnp.bfloat16)
        pick_low = jnp.where(slot == to_low, 1.0, 0.0).astype(jnp.bfloat16)
        message[s, 0] = (dot_nt(high, pick_high) + dot_nt(low, pick_low)).astype(jnp.bfloat16)
        message[s, 1] = panel
        return carry


    def field_copy(d):
        return pltpu.make_async_remote_copy(
            src_ref=own, dst_ref=fields.at[slab],
            send_sem=field_send.at[d], recv_sem=field_recv.at[d],
            device_id={"slab": lax.rem(slab + d, slabs)},
            device_id_type=pl.DeviceIdType.MESH,
        )

    def message_copy(d):
        to_shot = lax.rem(shot + d, shots)
        return pltpu.make_async_remote_copy(
            src_ref=message.at[to_shot], dst_ref=gathered.at[slab, shot],
            send_sem=send_sem.at[d], recv_sem=recv_sem.at[d],
            device_id={"shot": to_shot},
            device_id_type=pl.DeviceIdType.MESH,
        )

    def start_message(d, carry):
        fill(d, carry)
        message_copy(d).start()
        return carry

    def start_field(d, carry):
        field_copy(d).start()
        return carry

    def wait_field(d, carry):
        field_copy(d).wait()
        return carry

    def relay_copy(d, e):
        from_shot = lax.rem(shot + shots - d, shots)
        return pltpu.make_async_remote_copy(
            src_ref=gathered.at[slab, from_shot], dst_ref=gathered.at[slab, from_shot],
            send_sem=relay_send.at[e, d], recv_sem=relay_recv.at[e, d],
            device_id={"slab": lax.rem(slab + e, slabs)},
            device_id_type=pl.DeviceIdType.MESH,
        )

    def relay(d, carry):
        def one(e, inner):
            relay_copy(d, e).start()
            return inner

        return lax.fori_loop(1, slabs, one, carry)

    def arrive(d, carry):
        message_copy(d).wait_recv()
        return relay(d, carry)

    def finish(d, carry):
        def one(e, inner):
            relay_copy(d, e).wait()
            return inner

        return lax.fori_loop(1, slabs, one, carry)

    def sent(d, carry):
        message_copy(d).wait_send()
        return carry

    keep_message = pltpu.make_async_copy(
        message.at[shot], gathered.at[slab, shot], load_sem.at[0]
    )
    keep_field = pltpu.make_async_copy(own, fields.at[slab], load_sem.at[1])
    pl.semaphore_wait(barrier, shots - 1 + slabs - 1)
    lax.fori_loop(1, shots, start_message, 0, unroll=shots <= 8)
    fill(0, 0)
    keep_message.start()
    for load in loads[5:]:
        load.wait()
    for r in range(depth):
        to = (r % groups) * SUB + r // groups
        own[0, to : to + 1, :] = now_ref[r : r + 1, :]
        own[1, to : to + 1, :] = before_ref[r : r + 1, :]
    keep_field.start()
    lax.fori_loop(1, slabs, start_field, 0)
    keep_message.wait()
    relay(0, 0)
    lax.fori_loop(1, shots, arrive, 0)
    keep_field.wait()
    lax.fori_loop(1, slabs, wait_field, 0)
    lax.fori_loop(1, shots, sent, 0)
    lax.fori_loop(0, shots, finish, 0)


def wave_kernel(
    shots, slabs, offset_ref, source_ref, gathered_hbm, fields_hbm, out_ref,
    injection, left, right, courant, first, second, gathered, load_sem,
):
    depth, width = out_ref.shape
    groups = depth // SUB
    columns = width // LANES
    slab = lax.axis_index("slab")
    few = slabs <= 2

    load_gathered = pltpu.make_async_copy(gathered_hbm, gathered, load_sem.at[0])
    load_first = pltpu.make_async_copy(fields_hbm.at[:, 0], first, load_sem.at[1])
    load_second = pltpu.make_async_copy(fields_hbm.at[:, 1], second, load_sem.at[2])
    load_gathered.start()
    load_first.start()
    load_second.start()
    load_gathered.wait()
    lane = lax.broadcasted_iota(jnp.int32, (SUB, LANES), 1)
    sub = lax.broadcasted_iota(jnp.int32, (SUB, LANES), 0)
    offset = offset_ref[0]
    panel0 = offset // LANES
    shift = offset % LANES
    keep = lax.broadcasted_iota(jnp.int32, (depth, LANES), 1) < LANES - shift
    at_row = lax.broadcasted_iota(jnp.int32, (depth, LANES), 0)
    row_depth = ((at_row % SUB) * groups + at_row // SUB).astype(jnp.float32)
    at_cell = lax.broadcasted_iota(jnp.int32, (width, LANES), 0).astype(jnp.float32)

    def prepare(j, carry):
        turned = []
        for c in range(columns + 1):
            panel = jnp.minimum(panel0 + c, shots - 1)
            turned.append(
                pltpu.roll(
                    gathered[j, panel, 1].astype(jnp.float32), lax.rem(LANES - shift, LANES), 1
                )
            )
        for c in range(columns):
            window = jnp.where(keep, turned[c], turned[c + 1]) * RATIO
            courant[j, :, c * LANES : (c + 1) * LANES] = window * window

        def source(s, inner):
            lanes = pl.ds(pl.multiple_of(s * LANES, LANES), LANES)
            values = gathered[j, s, 0].astype(jnp.float32)
            at_depth = values[STEPS : STEPS + 1]
            at_lateral = values[STEPS + 1 : STEPS + 2] * 256.0 + values[STEPS + 2 : STEPS + 3]
            chosen = row_depth == at_depth
            for t in range(STEPS):
                left[t * depth : (t + 1) * depth, lanes] = jnp.where(
                    chosen, values[t : t + 1], 0.0
                ).astype(jnp.bfloat16)
            right[:, lanes] = jnp.where(at_cell == at_lateral, 1.0, 0.0).astype(jnp.bfloat16)
            return inner

        lax.fori_loop(0, shots, source, 0, unroll=shots <= 8)
        injection[j] = dot_nt(left[...], right[...])
        return carry

    lax.fori_loop(0, slabs, prepare, 0, unroll=few)

    source = source_ref[0]
    source_depth = source // width
    source_slab = source_depth // depth
    within = source_depth % depth
    source_row = (within % groups) * SUB + within // groups
    here = lax.broadcasted_iota(jnp.int32, (1, width), 1) == source % width
    for t in range(STEPS):
        spot = pl.ds(t * depth + source_row, 1)
        injection[source_slab, spot, :] = injection[source_slab, spot, :] + jnp.where(
            here, ricker_value(float(t)), 0.0
        )

    load_first.wait()
    load_second.wait()

    def step(t, now, other):
        def one_slab(j, carry):
            def cell(jj, v, c):
                return now[jj, v * SUB : (v + 1) * SUB, c * LANES : (c + 1) * LANES]

            up_ok = jnp.where(j + 1 < slabs, 1.0, 0.0) if not few else None
            down_ok = jnp.where(j > 0, 1.0, 0.0) if not few else None

            def ups(v, c):
                base = pltpu.roll(cell(j, v, c), SUB - 1, 0)
                if few:
                    beyond = pltpu.roll(cell(j + 1, v, c), SUB - 1, 0) if j + 1 < slabs else 0.0
                else:
                    beyond = pltpu.roll(cell(jnp.minimum(j + 1, slabs - 1), v, c), SUB - 1, 0)
                    beyond = beyond * up_ok
                return jnp.where(sub == SUB - 1, beyond, base)

            def downs(v, c):
                base = pltpu.roll(cell(j, v, c), 1, 0)
                if few:
                    beyond = pltpu.roll(cell(j - 1, v, c), 1, 0) if j > 0 else 0.0
                else:
                    beyond = pltpu.roll(cell(jnp.maximum(j - 1, 0), v, c), 1, 0) * down_ok
                return jnp.where(sub == 0, beyond, base)

            up = [[ups(v, c) for c in range(columns)] for v in range(groups)]
            down = [[downs(v, c) for c in range(columns)] for v in range(groups)]
            for v in range(groups):
                line = [cell(j, v, c) for c in range(columns)]
                totals = [LAP_CENTER * 2.0 * line[c] for c in range(columns)]
                for k in range(1, 5):
                    plus = [pltpu.roll(line[c], LANES - k, 1) for c in range(columns)]
                    minus = [pltpu.roll(line[c], k, 1) for c in range(columns)]
                    for c in range(columns):
                        after = plus[c + 1] if c + 1 < columns else 0.0
                        prior = minus[c - 1] if c > 0 else 0.0
                        sides = jnp.where(lane < LANES - k, plus[c], after) + jnp.where(
                            lane < k, prior, minus[c]
                        )
                        below = cell(j, v + k, c) if v + k < groups else up[v + k - groups][c]
                        above = cell(j, v - k, c) if v >= k else down[v - k + groups][c]
                        totals[c] = totals[c] + LAP_TAPS[k - 1] * (sides + (below + above))
                for c in range(columns):
                    rows = slice(v * SUB, (v + 1) * SUB)
                    lanes = slice(c * LANES, (c + 1) * LANES)
                    start = pl.multiple_of(t * depth + v * SUB, SUB)
                    other[j, rows, lanes] = (
                        2.0 * line[c]
                        - other[j, rows, lanes]
                        + courant[j, rows, lanes] * totals[c]
                        + injection[j, pl.ds(start, SUB), lanes]
                    )
            return carry

        if few:
            for j in range(slabs):
                one_slab(j, 0)
        else:
            lax.fori_loop(0, slabs, one_slab, 0)

    def pair(i, carry):
        step(2 * i, first, second)
        step(2 * i + 1, second, first)
        return carry

    lax.fori_loop(0, STEPS // 2, pair, 0)
    for r in range(depth):
        at = (r % groups) * SUB + r // groups
        out_ref[r : r + 1, :] = first[slab, at : at + 1, :]


def local(
    field_now, field_before, velocity, offsets, source_cell, traces, trace_shot, trace_node_cell
):
    depth, width = field_now.shape
    shots, slabs = lax.axis_size("shot"), lax.axis_size("slab")
    rows = traces.shape[1]
    vmem = pl.BlockSpec(memory_space=pltpu.VMEM)
    hbm = pl.BlockSpec(memory_space=pltpu.HBM)
    smem = pl.BlockSpec(memory_space=pltpu.SMEM)
    def exchange(*refs):
        exchange_kernel(shots, slabs, *refs)

    def wave(*refs):
        wave_kernel(shots, slabs, *refs)

    gathered, fields = pl.pallas_call(
        exchange,
        out_shape=(
            jax.ShapeDtypeStruct((slabs, shots, 2, depth, LANES), jnp.bfloat16),
            jax.ShapeDtypeStruct((slabs, 2, depth, width), jnp.float32),
        ),
        in_specs=[hbm] * 7,
        out_specs=(hbm, hbm),
        scratch_shapes=[
            pltpu.VMEM((shots, 2, depth, LANES), jnp.bfloat16),
            pltpu.VMEM((2, depth, width), jnp.float32),
            pltpu.SemaphoreType.DMA((shots,)),
            pltpu.SemaphoreType.DMA((shots,)),
            pltpu.SemaphoreType.DMA((slabs,)),
            pltpu.SemaphoreType.DMA((slabs,)),
            pltpu.SemaphoreType.DMA((slabs, shots)),
            pltpu.SemaphoreType.DMA((slabs, shots)),
            pltpu.VMEM((3 * ROWS, NS), jnp.bfloat16),
            pltpu.VMEM((depth, width), jnp.float32),
            pltpu.VMEM((depth, width), jnp.float32),
            pltpu.VMEM(velocity.shape, jnp.bfloat16),
            pltpu.VMEM((rows, NS), jnp.bfloat16),
            pltpu.VMEM((1, rows), jnp.int32),
            pltpu.VMEM((1, rows), jnp.int32),
            pltpu.SemaphoreType.DMA((7,)),
        ],
        compiler_params=pltpu.CompilerParams(
            collective_id=0, has_side_effects=True, vmem_limit_bytes=63 << 20
        ),
    )(
        split_table(), field_now, field_before, velocity, traces[0],
        trace_shot.reshape(1, rows), trace_node_cell,
    )
    return pl.pallas_call(
        wave,
        out_shape=jax.ShapeDtypeStruct((depth, width), jnp.float32),
        in_specs=[smem, smem, hbm, hbm],
        out_specs=vmem,
        scratch_shapes=[
            pltpu.VMEM((slabs, STEPS * depth, width), jnp.float32),
            pltpu.VMEM((STEPS * depth, shots * LANES), jnp.bfloat16),
            pltpu.VMEM((width, shots * LANES), jnp.bfloat16),
            pltpu.VMEM((slabs, depth, width), jnp.float32),
            pltpu.VMEM((slabs, depth, width), jnp.float32),
            pltpu.VMEM((slabs, depth, width), jnp.float32),
            pltpu.VMEM((slabs, shots, 2, depth, LANES), jnp.bfloat16),
            pltpu.SemaphoreType.DMA((3,)),
        ],
        compiler_params=pltpu.CompilerParams(vmem_limit_bytes=63 << 20),
    )(offsets, source_cell, gathered, fields)


def solution(mesh):
    in_specs = (
        P("slab", ("groups", "shot")),
        P("slab", ("groups", "shot")),
        P("slab", ("groups", "shot")),
        P(("groups", "shot")),
        P(("groups", "shot")),
        P("slab", ("groups", "shot"), None),
        P("slab", ("groups", "shot"), None),
        P("slab", ("groups", "shot")),
    )
    out_specs = P("slab", ("groups", "shot"))
    return jax.shard_map(local, mesh=mesh, in_specs=in_specs, out_specs=out_specs, check_vma=False)
```

```python
import math

import jax
import jax.numpy as jnp
import numpy as np
from jax import lax
from jax.experimental import pallas as pl
from jax.experimental.pallas import tpu as pltpu
from jax.sharding import PartitionSpec as P

NS = 256
STEPS = 24
CAP = 64
LANES = 128
SUB = 8
ROWS = 32

LAP_CENTER = -205.0 / 72.0
LAP_TAPS = (1.6, -0.2, 8.0 / 315.0, -1.0 / 560.0)
PEAK = 0.12
DELAY = 5.0
SOURCE_GAIN = 2.0
RATIO = 0.1
NT = (((1,), (1,)), ((), ()))


def dot_nt(a, b):
    return lax.dot_general(a, b, NT, preferred_element_type=jnp.float32)


def split_table():
    k = np.arange(NS, dtype=np.float64)[:, None] + 0.5
    t = np.arange(STEPS, dtype=np.float64)[None, :] + 1.0
    table = np.cos(math.pi * k * t / NS) * math.sqrt(2.0 / NS)
    rest = np.zeros((ROWS, NS), np.float32)
    rest[:STEPS] = table.T
    parts = []
    for _ in range(3):
        part = rest.astype(jnp.bfloat16)
        parts.append(part)
        rest = rest - part.astype(np.float32)
    return jnp.asarray(np.concatenate(parts, axis=0))


def ricker_value(step):
    a = (math.pi * PEAK * (step - DELAY)) ** 2
    return SOURCE_GAIN * (1.0 - 2.0 * a) * math.exp(-a)


def exchange_kernel(
    shots, slabs, table_hbm, now_hbm, before_hbm, velocity_hbm, traces_hbm, shot_hbm, node_hbm,
    gathered, fields, message, own, send_sem, recv_sem, field_send, field_recv, relay_send, relay_recv,
    table_ref, now_ref, before_ref, velocity_ref, traces_ref, shot_ref, node_ref, load_sem,
):
    shot, slab = lax.axis_index("shot"), lax.axis_index("slab")
    depth, width = now_ref.shape
    groups = depth // SUB
    rows = traces_ref.shape[0]

    loads = [
        pltpu.make_async_copy(source, to, load_sem.at[i])
        for i, (source, to) in enumerate(
            (
                (traces_hbm, traces_ref), (shot_hbm, shot_ref), (node_hbm, node_ref),
                (table_hbm, table_ref), (velocity_hbm, velocity_ref),
                (now_hbm, now_ref), (before_hbm, before_ref),
            )
        )
    ]
    for load in loads:
        load.start()

    barrier = pltpu.get_barrier_semaphore()

    def greet_shot(d, carry):
        pl.semaphore_signal(
            barrier, inc=1, device_id={"shot": lax.rem(shot + d, shots)},
            device_id_type=pl.DeviceIdType.MESH,
        )
        return carry

    def greet_slab(d, carry):
        pl.semaphore_signal(
            barrier, inc=1, device_id={"slab": lax.rem(slab + d, slabs)},
            device_id_type=pl.DeviceIdType.MESH,
        )
        return carry

    lax.fori_loop(1, shots, greet_shot, 0)
    lax.fori_loop(1, slabs, greet_slab, 0)

    for load in loads[:5]:
        load.wait()
    parts = dot_nt(table_ref[...], traces_ref[...])
    amplitude = parts[0:ROWS] + parts[ROWS : 2 * ROWS] + parts[2 * ROWS : 3 * ROWS]
    node = node_ref[...]
    lateral = node % width
    row = lax.broadcasted_iota(jnp.int32, (ROWS, rows), 0)
    where_to = jnp.where(
        row == STEPS, node // width, jnp.where(row == STEPS + 1, lateral // 256, lateral % 256)
    ).astype(jnp.float32)
    high = jnp.where(row < STEPS, amplitude, where_to).astype(jnp.bfloat16)
    low = jnp.where(row < STEPS, amplitude - high.astype(jnp.float32), where_to).astype(
        jnp.bfloat16
    )
    target = shot_ref[...]
    chosen = lax.broadcasted_iota(jnp.int32, (shots, rows), 0) == target
    onehot = jnp.where(chosen, 1.0, 0.0)
    ahead = jnp.where(
        lax.broadcasted_iota(jnp.int32, (rows, rows), 0)
        < lax.broadcasted_iota(jnp.int32, (rows, rows), 1),
        1.0, 0.0,
    ).astype(jnp.bfloat16)
    count = jnp.dot(onehot.astype(jnp.bfloat16), ahead, preferred_element_type=jnp.float32)
    position = jnp.sum(onehot * count, axis=0, keepdims=True)
    slot = lax.broadcasted_iota(jnp.int32, (LANES, rows), 0).astype(jnp.float32)

    turn = lax.broadcasted_iota(jnp.int32, (depth, depth), 0)
    turned = jnp.where(
        (turn % SUB) * groups + turn // SUB
        == lax.broadcasted_iota(jnp.int32, (depth, depth), 1),
        1.0, 0.0,
    ).astype(jnp.bfloat16)
    panel = jnp.dot(turned, velocity_ref[...], preferred_element_type=jnp.float32).astype(
        jnp.bfloat16
    )

    def fill(d, carry):
        s = lax.rem(shot + d, shots)
        mine = target == s
        to_high = jnp.where(mine, position, -1.0)
        to_low = jnp.where(mine, position + float(CAP), -1.0)
        pick_high = jnp.where(slot == to_high, 1.0, 0.0).astype(jnp.bfloat16)
        pick_low = jnp.where(slot == to_low, 1.0, 0.0).astype(jnp.bfloat16)
        message[s, 0] = (dot_nt(high, pick_high) + dot_nt(low, pick_low)).astype(jnp.bfloat16)
        message[s, 1] = panel
        return carry


    def field_copy(d):
        return pltpu.make_async_remote_copy(
            src_ref=own, dst_ref=fields.at[slab],
            send_sem=field_send.at[d], recv_sem=field_recv.at[d],
            device_id={"slab": lax.rem(slab + d, slabs)},
            device_id_type=pl.DeviceIdType.MESH,
        )

    def message_copy(d):
        to_shot = lax.rem(shot + d, shots)
        return pltpu.make_async_remote_copy(
            src_ref=message.at[to_shot], dst_ref=gathered.at[slab, shot],
            send_sem=send_sem.at[d], recv_sem=recv_sem.at[d],
            device_id={"shot": to_shot},
            device_id_type=pl.DeviceIdType.MESH,
        )

    def start_message(d, carry):
        fill(d, carry)
        message_copy(d).start()
        return carry

    def start_field(d, carry):
        field_copy(d).start()
        return carry

    def wait_field(d, carry):
        field_copy(d).wait()
        return carry

    def relay_copy(d, e):
        from_shot = lax.rem(shot + shots - d, shots)
        return pltpu.make_async_remote_copy(
            src_ref=gathered.at[slab, from_shot], dst_ref=gathered.at[slab, from_shot],
            send_sem=relay_send.at[e, d], recv_sem=relay_recv.at[e, d],
            device_id={"slab": lax.rem(slab + e, slabs)},
            device_id_type=pl.DeviceIdType.MESH,
        )

    def relay(d, carry):
        def one(e, inner):
            relay_copy(d, e).start()
            return inner

        return lax.fori_loop(1, slabs, one, carry)

    def arrive(d, carry):
        message_copy(d).wait_recv()
        return relay(d, carry)

    def finish(d, carry):
        def one(e, inner):
            relay_copy(d, e).wait()
            return inner

        return lax.fori_loop(1, slabs, one, carry)

    def sent(d, carry):
        message_copy(d).wait_send()
        return carry

    keep_message = pltpu.make_async_copy(
        message.at[shot], gathered.at[slab, shot], load_sem.at[0]
    )
    keep_field = pltpu.make_async_copy(own, fields.at[slab], load_sem.at[1])
    pl.semaphore_wait(barrier, shots - 1 + slabs - 1)
    lax.fori_loop(1, shots, start_message, 0, unroll=shots <= 8)
    fill(0, 0)
    keep_message.start()
    for load in loads[5:]:
        load.wait()
    for r in range(depth):
        to = (r % groups) * SUB + r // groups
        own[0, to : to + 1, :] = now_ref[r : r + 1, :]
        own[1, to : to + 1, :] = before_ref[r : r + 1, :]
    keep_field.start()
    lax.fori_loop(1, slabs, start_field, 0)
    keep_message.wait()
    relay(0, 0)
    lax.fori_loop(1, shots, arrive, 0)
    keep_field.wait()
    lax.fori_loop(1, slabs, wait_field, 0)
    lax.fori_loop(1, shots, sent, 0)
    lax.fori_loop(0, shots, finish, 0)


def wave_kernel(
    shots, slabs, offset_ref, source_ref, gathered_hbm, fields_hbm, out_ref,
    injection, left, right, courant, first, second, gathered, load_sem,
):
    depth, width = out_ref.shape
    groups = depth // SUB
    columns = width // LANES
    slab = lax.axis_index("slab")
    few = slabs <= 2

    load_gathered = pltpu.make_async_copy(gathered_hbm, gathered, load_sem.at[0])
    load_first = pltpu.make_async_copy(fields_hbm.at[:, 0], first, load_sem.at[1])
    load_second = pltpu.make_async_copy(fields_hbm.at[:, 1], second, load_sem.at[2])
    load_gathered.start()
    load_first.start()
    load_second.start()
    load_gathered.wait()
    lane = lax.broadcasted_iota(jnp.int32, (SUB, LANES), 1)
    sub = lax.broadcasted_iota(jnp.int32, (SUB, LANES), 0)
    offset = offset_ref[0]
    panel0 = offset // LANES
    shift = offset % LANES
    keep = lax.broadcasted_iota(jnp.int32, (depth, LANES), 1) < LANES - shift
    at_row = lax.broadcasted_iota(jnp.int32, (depth, LANES), 0)
    row_depth = ((at_row % SUB) * groups + at_row // SUB).astype(jnp.float32)
    at_cell = lax.broadcasted_iota(jnp.int32, (width, LANES), 0).astype(jnp.float32)

    def prepare(j, carry):
        half = j % 2
        turned = []
        for c in range(columns + 1):
            panel = jnp.minimum(panel0 + c, shots - 1)
            turned.append(
                pltpu.roll(
                    gathered[j, panel, 1].astype(jnp.float32), lax.rem(LANES - shift, LANES), 1
                )
            )
        for c in range(columns):
            window = jnp.where(keep, turned[c], turned[c + 1]) * RATIO
            courant[j, :, c * LANES : (c + 1) * LANES] = window * window

        def source(s, inner):
            lanes = pl.ds(pl.multiple_of(s * LANES, LANES), LANES)
            values = gathered[j, s, 0].astype(jnp.float32)
            at_depth = values[STEPS : STEPS + 1]
            at_lateral = values[STEPS + 1 : STEPS + 2] * 256.0 + values[STEPS + 2 : STEPS + 3]
            chosen = jnp.where(row_depth == at_depth, 1.0, 0.0).astype(jnp.bfloat16)
            for t in range(STEPS):
                spread = jnp.broadcast_to(values[t : t + 1], (2 * SUB, LANES)).astype(
                    jnp.bfloat16
                )
                for part in range(0, depth, 2 * SUB):
                    left[half, t * depth + part : t * depth + part + 2 * SUB, lanes] = (
                        chosen[part : part + 2 * SUB] * spread
                    )
            right[half, :, lanes] = jnp.where(at_cell == at_lateral, 1.0, 0.0).astype(jnp.bfloat16)
            return inner

        lax.fori_loop(0, shots, source, 0, unroll=shots <= 8)
        injection[j] = dot_nt(left[half], right[half])
        return carry

    if few:
        for j in range(slabs):
            prepare(j, 0)
    else:
        lax.fori_loop(0, slabs, prepare, 0)

    source = source_ref[0]
    source_depth = source // width
    source_slab = source_depth // depth
    within = source_depth % depth
    source_row = (within % groups) * SUB + within // groups
    here = lax.broadcasted_iota(jnp.int32, (1, width), 1) == source % width
    for t in range(STEPS):
        spot = pl.ds(t * depth + source_row, 1)
        injection[source_slab, spot, :] = injection[source_slab, spot, :] + jnp.where(
            here, ricker_value(float(t)), 0.0
        )

    load_first.wait()
    load_second.wait()

    def step(t, now, other):
        def one_slab(j, carry):
            def cell(jj, v, c):
                return now[jj, v * SUB : (v + 1) * SUB, c * LANES : (c + 1) * LANES]

            up_ok = jnp.where(j + 1 < slabs, 1.0, 0.0) if not few else None
            down_ok = jnp.where(j > 0, 1.0, 0.0) if not few else None

            def ups(v, c):
                base = pltpu.roll(cell(j, v, c), SUB - 1, 0)
                if few:
                    beyond = pltpu.roll(cell(j + 1, v, c), SUB - 1, 0) if j + 1 < slabs else 0.0
                else:
                    beyond = pltpu.roll(cell(jnp.minimum(j + 1, slabs - 1), v, c), SUB - 1, 0)
                    beyond = beyond * up_ok
                return jnp.where(sub == SUB - 1, beyond, base)

            def downs(v, c):
                base = pltpu.roll(cell(j, v, c), 1, 0)
                if few:
                    beyond = pltpu.roll(cell(j - 1, v, c), 1, 0) if j > 0 else 0.0
                else:
                    beyond = pltpu.roll(cell(jnp.maximum(j - 1, 0), v, c), 1, 0) * down_ok
                return jnp.where(sub == 0, beyond, base)

            up = [[ups(v, c) for c in range(columns)] for v in range(groups)]
            down = [[downs(v, c) for c in range(columns)] for v in range(groups)]
            for v in range(groups):
                line = [cell(j, v, c) for c in range(columns)]
                totals = [LAP_CENTER * 2.0 * line[c] for c in range(columns)]
                for k in range(1, 5):
                    plus = [pltpu.roll(line[c], LANES - k, 1) for c in range(columns)]
                    minus = [pltpu.roll(line[c], k, 1) for c in range(columns)]
                    for c in range(columns):
                        after = plus[c + 1] if c + 1 < columns else 0.0
                        prior = minus[c - 1] if c > 0 else 0.0
                        sides = jnp.where(lane < LANES - k, plus[c], after) + jnp.where(
                            lane < k, prior, minus[c]
                        )
                        below = cell(j, v + k, c) if v + k < groups else up[v + k - groups][c]
                        above = cell(j, v - k, c) if v >= k else down[v - k + groups][c]
                        totals[c] = totals[c] + LAP_TAPS[k - 1] * (sides + (below + above))
                for c in range(columns):
                    rows = slice(v * SUB, (v + 1) * SUB)
                    lanes = slice(c * LANES, (c + 1) * LANES)
                    start = pl.multiple_of(t * depth + v * SUB, SUB)
                    other[j, rows, lanes] = (
                        2.0 * line[c]
                        - other[j, rows, lanes]
                        + courant[j, rows, lanes] * totals[c]
                        + injection[j, pl.ds(start, SUB), lanes]
                    )
            return carry

        if few:
            for j in range(slabs):
                one_slab(j, 0)
        else:
            lax.fori_loop(0, slabs, one_slab, 0)

    def pair(i, carry):
        step(2 * i, first, second)
        step(2 * i + 1, second, first)
        return carry

    lax.fori_loop(0, STEPS // 2, pair, 0, unroll=2)
    for r in range(depth):
        at = (r % groups) * SUB + r // groups
        out_ref[r : r + 1, :] = first[slab, at : at + 1, :]


def local(
    field_now, field_before, velocity, offsets, source_cell, traces, trace_shot, trace_node_cell
):
    depth, width = field_now.shape
    shots, slabs = lax.axis_size("shot"), lax.axis_size("slab")
    rows = traces.shape[1]
    vmem = pl.BlockSpec(memory_space=pltpu.VMEM)
    hbm = pl.BlockSpec(memory_space=pltpu.HBM)
    smem = pl.BlockSpec(memory_space=pltpu.SMEM)
    def exchange(*refs):
        exchange_kernel(shots, slabs, *refs)

    def wave(*refs):
        wave_kernel(shots, slabs, *refs)

    gathered, fields = pl.pallas_call(
        exchange,
        out_shape=(
            jax.ShapeDtypeStruct((slabs, shots, 2, depth, LANES), jnp.bfloat16),
            jax.ShapeDtypeStruct((slabs, 2, depth, width), jnp.float32),
        ),
        in_specs=[hbm] * 7,
        out_specs=(hbm, hbm),
        scratch_shapes=[
            pltpu.VMEM((shots, 2, depth, LANES), jnp.bfloat16),
            pltpu.VMEM((2, depth, width), jnp.float32),
            pltpu.SemaphoreType.DMA((shots,)),
            pltpu.SemaphoreType.DMA((shots,)),
            pltpu.SemaphoreType.DMA((slabs,)),
            pltpu.SemaphoreType.DMA((slabs,)),
            pltpu.SemaphoreType.DMA((slabs, shots)),
            pltpu.SemaphoreType.DMA((slabs, shots)),
            pltpu.VMEM((3 * ROWS, NS), jnp.bfloat16),
            pltpu.VMEM((depth, width), jnp.float32),
            pltpu.VMEM((depth, width), jnp.float32),
            pltpu.VMEM(velocity.shape, jnp.bfloat16),
            pltpu.VMEM((rows, NS), jnp.bfloat16),
            pltpu.VMEM((1, rows), jnp.int32),
            pltpu.VMEM((1, rows), jnp.int32),
            pltpu.SemaphoreType.DMA((7,)),
        ],
        compiler_params=pltpu.CompilerParams(
            collective_id=0, has_side_effects=True, vmem_limit_bytes=63 << 20
        ),
    )(
        split_table(), field_now, field_before, velocity, traces[0],
        trace_shot.reshape(1, rows), trace_node_cell,
    )
    return pl.pallas_call(
        wave,
        out_shape=jax.ShapeDtypeStruct((depth, width), jnp.float32),
        in_specs=[smem, smem, hbm, hbm],
        out_specs=vmem,
        scratch_shapes=[
            pltpu.VMEM((slabs, STEPS * depth, width), jnp.float32),
            pltpu.VMEM((2, STEPS * depth, shots * LANES), jnp.bfloat16),
            pltpu.VMEM((2, width, shots * LANES), jnp.bfloat16),
            pltpu.VMEM((slabs, depth, width), jnp.float32),
            pltpu.VMEM((slabs, depth, width), jnp.float32),
            pltpu.VMEM((slabs, depth, width), jnp.float32),
            pltpu.VMEM((slabs, shots, 2, depth, LANES), jnp.bfloat16),
            pltpu.SemaphoreType.DMA((3,)),
        ],
        compiler_params=pltpu.CompilerParams(vmem_limit_bytes=63 << 20),
    )(offsets, source_cell, gathered, fields)


def solution(mesh):
    in_specs = (
        P("slab", ("groups", "shot")),
        P("slab", ("groups", "shot")),
        P("slab", ("groups", "shot")),
        P(("groups", "shot")),
        P(("groups", "shot")),
        P("slab", ("groups", "shot"), None),
        P("slab", ("groups", "shot"), None),
        P("slab", ("groups", "shot")),
    )
    out_specs = P("slab", ("groups", "shot"))
    return jax.shard_map(local, mesh=mesh, in_specs=in_specs, out_specs=out_specs, check_vma=False)
```

```python
import math

import jax
import jax.numpy as jnp
import numpy as np
from jax import lax
from jax.experimental import pallas as pl
from jax.experimental.pallas import tpu as pltpu
from jax.sharding import PartitionSpec as P

NS = 256
STEPS = 24
CAP = 64
LANES = 128
SUB = 8
ROWS = 32

LAP_CENTER = -205.0 / 72.0
LAP_TAPS = (1.6, -0.2, 8.0 / 315.0, -1.0 / 560.0)
PEAK = 0.12
DELAY = 5.0
SOURCE_GAIN = 2.0
RATIO = 0.1
NT = (((1,), (1,)), ((), ()))


def dot_nt(a, b):
    return lax.dot_general(a, b, NT, preferred_element_type=jnp.float32)


def split_table():
    k = np.arange(NS, dtype=np.float64)[:, None] + 0.5
    t = np.arange(STEPS, dtype=np.float64)[None, :] + 1.0
    table = np.cos(math.pi * k * t / NS) * math.sqrt(2.0 / NS)
    rest = np.zeros((ROWS, NS), np.float32)
    rest[:STEPS] = table.T
    parts = []
    for _ in range(3):
        part = rest.astype(jnp.bfloat16)
        parts.append(part)
        rest = rest - part.astype(np.float32)
    return jnp.asarray(np.concatenate(parts, axis=0))


def ricker_value(step):
    a = (math.pi * PEAK * (step - DELAY)) ** 2
    return SOURCE_GAIN * (1.0 - 2.0 * a) * math.exp(-a)


def exchange_kernel(
    shots, slabs, table_hbm, now_hbm, before_hbm, velocity_hbm, traces_hbm, shot_hbm, node_hbm,
    gathered, fields, message, own, send_sem, recv_sem, field_send, field_recv, relay_send, relay_recv,
    table_ref, now_ref, before_ref, velocity_ref, traces_ref, shot_ref, node_ref, load_sem,
):
    shot, slab = lax.axis_index("shot"), lax.axis_index("slab")
    depth, width = now_ref.shape
    groups = depth // SUB
    rows = traces_ref.shape[0]

    loads = [
        pltpu.make_async_copy(source, to, load_sem.at[i])
        for i, (source, to) in enumerate(
            (
                (traces_hbm, traces_ref), (shot_hbm, shot_ref), (node_hbm, node_ref),
                (table_hbm, table_ref), (velocity_hbm, velocity_ref),
                (now_hbm, now_ref), (before_hbm, before_ref),
            )
        )
    ]
    for load in loads:
        load.start()

    barrier = pltpu.get_barrier_semaphore()

    def greet_shot(d, carry):
        pl.semaphore_signal(
            barrier, inc=1, device_id={"shot": lax.rem(shot + d, shots)},
            device_id_type=pl.DeviceIdType.MESH,
        )
        return carry

    def greet_slab(d, carry):
        pl.semaphore_signal(
            barrier, inc=1, device_id={"slab": lax.rem(slab + d, slabs)},
            device_id_type=pl.DeviceIdType.MESH,
        )
        return carry

    lax.fori_loop(1, shots, greet_shot, 0)
    lax.fori_loop(1, slabs, greet_slab, 0)

    for load in loads[:5]:
        load.wait()
    parts = dot_nt(table_ref[...], traces_ref[...])
    amplitude = parts[0:ROWS] + parts[ROWS : 2 * ROWS] + parts[2 * ROWS : 3 * ROWS]
    node = node_ref[...]
    lateral = node % width
    row = lax.broadcasted_iota(jnp.int32, (ROWS, rows), 0)
    where_to = jnp.where(
        row == STEPS, node // width, jnp.where(row == STEPS + 1, lateral // 256, lateral % 256)
    ).astype(jnp.float32)
    high = jnp.where(row < STEPS, amplitude, where_to).astype(jnp.bfloat16)
    low = jnp.where(row < STEPS, amplitude - high.astype(jnp.float32), where_to).astype(
        jnp.bfloat16
    )
    target = shot_ref[...]
    chosen = lax.broadcasted_iota(jnp.int32, (shots, rows), 0) == target
    onehot = jnp.where(chosen, 1.0, 0.0)
    ahead = jnp.where(
        lax.broadcasted_iota(jnp.int32, (rows, rows), 0)
        < lax.broadcasted_iota(jnp.int32, (rows, rows), 1),
        1.0, 0.0,
    ).astype(jnp.bfloat16)
    count = jnp.dot(onehot.astype(jnp.bfloat16), ahead, preferred_element_type=jnp.float32)
    position = jnp.sum(onehot * count, axis=0, keepdims=True)
    slot = lax.broadcasted_iota(jnp.int32, (LANES, rows), 0).astype(jnp.float32)

    turn = lax.broadcasted_iota(jnp.int32, (depth, depth), 0)
    turned = jnp.where(
        (turn % SUB) * groups + turn // SUB
        == lax.broadcasted_iota(jnp.int32, (depth, depth), 1),
        1.0, 0.0,
    ).astype(jnp.bfloat16)
    panel = jnp.dot(turned, velocity_ref[...], preferred_element_type=jnp.float32).astype(
        jnp.bfloat16
    )

    def fill(d, carry):
        s = lax.rem(shot + d, shots)
        mine = target == s
        to_high = jnp.where(mine, position, -1.0)
        to_low = jnp.where(mine, position + float(CAP), -1.0)
        pick_high = jnp.where(slot == to_high, 1.0, 0.0).astype(jnp.bfloat16)
        pick_low = jnp.where(slot == to_low, 1.0, 0.0).astype(jnp.bfloat16)
        message[s, 0] = (dot_nt(high, pick_high) + dot_nt(low, pick_low)).astype(jnp.bfloat16)
        message[s, 1] = panel
        return carry


    def field_copy(d):
        return pltpu.make_async_remote_copy(
            src_ref=own, dst_ref=fields.at[slab],
            send_sem=field_send.at[d], recv_sem=field_recv.at[d],
            device_id={"slab": lax.rem(slab + d, slabs)},
            device_id_type=pl.DeviceIdType.MESH,
        )

    def message_copy(d):
        to_shot = lax.rem(shot + d, shots)
        return pltpu.make_async_remote_copy(
            src_ref=message.at[to_shot], dst_ref=gathered.at[slab, shot],
            send_sem=send_sem.at[d], recv_sem=recv_sem.at[d],
            device_id={"shot": to_shot},
            device_id_type=pl.DeviceIdType.MESH,
        )

    def start_message(d, carry):
        fill(d, carry)
        message_copy(d).start()
        return carry

    def start_field(d, carry):
        field_copy(d).start()
        return carry

    def wait_field(d, carry):
        field_copy(d).wait()
        return carry

    def relay_copy(d, e):
        from_shot = lax.rem(shot + shots - d, shots)
        return pltpu.make_async_remote_copy(
            src_ref=gathered.at[slab, from_shot], dst_ref=gathered.at[slab, from_shot],
            send_sem=relay_send.at[e, d], recv_sem=relay_recv.at[e, d],
            device_id={"slab": lax.rem(slab + e, slabs)},
            device_id_type=pl.DeviceIdType.MESH,
        )

    def relay(d, carry):
        def one(e, inner):
            relay_copy(d, e).start()
            return inner

        return lax.fori_loop(1, slabs, one, carry)

    def arrive(d, carry):
        message_copy(d).wait_recv()
        return relay(d, carry)

    def finish(d, carry):
        def one(e, inner):
            relay_copy(d, e).wait()
            return inner

        return lax.fori_loop(1, slabs, one, carry)

    def sent(d, carry):
        message_copy(d).wait_send()
        return carry

    keep_message = pltpu.make_async_copy(
        message.at[shot], gathered.at[slab, shot], load_sem.at[0]
    )
    keep_field = pltpu.make_async_copy(own, fields.at[slab], load_sem.at[1])
    pl.semaphore_wait(barrier, shots - 1 + slabs - 1)
    lax.fori_loop(1, shots, start_message, 0, unroll=shots <= 8)
    fill(0, 0)
    keep_message.start()
    for load in loads[5:]:
        load.wait()
    for r in range(depth):
        to = (r % groups) * SUB + r // groups
        own[0, to : to + 1, :] = now_ref[r : r + 1, :]
        own[1, to : to + 1, :] = before_ref[r : r + 1, :]
    keep_field.start()
    lax.fori_loop(1, slabs, start_field, 0)
    keep_message.wait()
    relay(0, 0)
    lax.fori_loop(1, shots, arrive, 0)
    keep_field.wait()
    lax.fori_loop(1, slabs, wait_field, 0)
    lax.fori_loop(1, shots, sent, 0)
    lax.fori_loop(0, shots, finish, 0)


def wave_kernel(
    shots, slabs, offset_ref, source_ref, gathered_hbm, fields_hbm, out_ref,
    injection, left, right, courant, first, second, gathered, load_sem,
):
    depth, width = out_ref.shape
    groups = depth // SUB
    columns = width // LANES
    slab = lax.axis_index("slab")
    few = slabs <= 2

    load_gathered = pltpu.make_async_copy(gathered_hbm, gathered, load_sem.at[0])
    load_first = pltpu.make_async_copy(fields_hbm.at[:, 0], first, load_sem.at[1])
    load_second = pltpu.make_async_copy(fields_hbm.at[:, 1], second, load_sem.at[2])
    load_gathered.start()
    load_first.start()
    load_second.start()
    load_gathered.wait()
    lane = lax.broadcasted_iota(jnp.int32, (SUB, LANES), 1)
    sub = lax.broadcasted_iota(jnp.int32, (SUB, LANES), 0)
    offset = offset_ref[0]
    panel0 = offset // LANES
    shift = offset % LANES
    keep = lax.broadcasted_iota(jnp.int32, (depth, LANES), 1) < LANES - shift
    at_row = lax.broadcasted_iota(jnp.int32, (depth, LANES), 0)
    row_depth = ((at_row % SUB) * groups + at_row // SUB).astype(jnp.float32)
    at_cell = lax.broadcasted_iota(jnp.int32, (width, LANES), 0).astype(jnp.float32)

    def prepare(j, carry):
        half = j % 2
        turned = []
        for c in range(columns + 1):
            panel = jnp.minimum(panel0 + c, shots - 1)
            turned.append(
                pltpu.roll(
                    gathered[j, panel, 1].astype(jnp.float32), lax.rem(LANES - shift, LANES), 1
                )
            )
        for c in range(columns):
            window = jnp.where(keep, turned[c], turned[c + 1]) * RATIO
            courant[j, :, c * LANES : (c + 1) * LANES] = window * window

        def source(s, inner):
            lanes = pl.ds(pl.multiple_of(s * LANES, LANES), LANES)
            values = gathered[j, s, 0].astype(jnp.float32)
            at_depth = values[STEPS : STEPS + 1]
            at_lateral = values[STEPS + 1 : STEPS + 2] * 256.0 + values[STEPS + 2 : STEPS + 3]
            chosen = jnp.where(row_depth == at_depth, 1.0, 0.0).astype(jnp.bfloat16)
            for t in range(STEPS):
                spread = jnp.broadcast_to(values[t : t + 1], (2 * SUB, LANES)).astype(
                    jnp.bfloat16
                )
                for part in range(0, depth, 2 * SUB):
                    left[half, t * depth + part : t * depth + part + 2 * SUB, lanes] = (
                        chosen[part : part + 2 * SUB] * spread
                    )
            right[half, :, lanes] = jnp.where(at_cell == at_lateral, 1.0, 0.0).astype(jnp.bfloat16)
            return inner

        lax.fori_loop(0, shots, source, 0, unroll=shots <= 8)
        injection[j] = dot_nt(left[half], right[half])
        return carry

    if few:
        for j in range(slabs):
            prepare(j, 0)
    else:
        lax.fori_loop(0, slabs, prepare, 0)

    source = source_ref[0]
    source_depth = source // width
    source_slab = source_depth // depth
    within = source_depth % depth
    source_row = (within % groups) * SUB + within // groups
    here = lax.broadcasted_iota(jnp.int32, (1, width), 1) == source % width
    for t in range(STEPS):
        spot = pl.ds(t * depth + source_row, 1)
        injection[source_slab, spot, :] = injection[source_slab, spot, :] + jnp.where(
            here, ricker_value(float(t)), 0.0
        )

    load_first.wait()
    load_second.wait()

    def step(t, now, other):
        def one_slab(j, carry):
            def cell(jj, v, c):
                return now[jj, v * SUB : (v + 1) * SUB, c * LANES : (c + 1) * LANES]

            up_ok = jnp.where(j + 1 < slabs, 1.0, 0.0) if not few else None
            down_ok = jnp.where(j > 0, 1.0, 0.0) if not few else None

            def ups(v, c):
                base = pltpu.roll(cell(j, v, c), SUB - 1, 0)
                if few:
                    beyond = pltpu.roll(cell(j + 1, v, c), SUB - 1, 0) if j + 1 < slabs else 0.0
                else:
                    beyond = pltpu.roll(cell(jnp.minimum(j + 1, slabs - 1), v, c), SUB - 1, 0)
                    beyond = beyond * up_ok
                return jnp.where(sub == SUB - 1, beyond, base)

            def downs(v, c):
                base = pltpu.roll(cell(j, v, c), 1, 0)
                if few:
                    beyond = pltpu.roll(cell(j - 1, v, c), 1, 0) if j > 0 else 0.0
                else:
                    beyond = pltpu.roll(cell(jnp.maximum(j - 1, 0), v, c), 1, 0) * down_ok
                return jnp.where(sub == 0, beyond, base)

            up = [[ups(v, c) for c in range(columns)] for v in range(groups)]
            down = [[downs(v, c) for c in range(columns)] for v in range(groups)]
            for v in range(groups):
                line = [cell(j, v, c) for c in range(columns)]
                totals = [LAP_CENTER * 2.0 * line[c] for c in range(columns)]
                for k in range(1, 5):
                    plus = [pltpu.roll(line[c], LANES - k, 1) for c in range(columns)]
                    minus = [pltpu.roll(line[c], k, 1) for c in range(columns)]
                    for c in range(columns):
                        after = plus[c + 1] if c + 1 < columns else 0.0
                        prior = minus[c - 1] if c > 0 else 0.0
                        sides = jnp.where(lane < LANES - k, plus[c], after) + jnp.where(
                            lane < k, prior, minus[c]
                        )
                        below = cell(j, v + k, c) if v + k < groups else up[v + k - groups][c]
                        above = cell(j, v - k, c) if v >= k else down[v - k + groups][c]
                        totals[c] = totals[c] + LAP_TAPS[k - 1] * (sides + (below + above))
                for c in range(columns):
                    rows = slice(v * SUB, (v + 1) * SUB)
                    lanes = slice(c * LANES, (c + 1) * LANES)
                    start = pl.multiple_of(t * depth + v * SUB, SUB)
                    other[j, rows, lanes] = (
                        2.0 * line[c]
                        - other[j, rows, lanes]
                        + courant[j, rows, lanes] * totals[c]
                        + injection[j, pl.ds(start, SUB), lanes]
                    )
            return carry

        if few:
            for j in range(slabs):
                one_slab(j, 0)
        else:
            lax.fori_loop(0, slabs, one_slab, 0)

    def pair(i, carry):
        step(2 * i, first, second)
        step(2 * i + 1, second, first)
        return carry

    lax.fori_loop(0, STEPS // 2, pair, 0, unroll=4)
    for r in range(depth):
        at = (r % groups) * SUB + r // groups
        out_ref[r : r + 1, :] = first[slab, at : at + 1, :]


def local(
    field_now, field_before, velocity, offsets, source_cell, traces, trace_shot, trace_node_cell
):
    depth, width = field_now.shape
    shots, slabs = lax.axis_size("shot"), lax.axis_size("slab")
    rows = traces.shape[1]
    vmem = pl.BlockSpec(memory_space=pltpu.VMEM)
    hbm = pl.BlockSpec(memory_space=pltpu.HBM)
    smem = pl.BlockSpec(memory_space=pltpu.SMEM)
    def exchange(*refs):
        exchange_kernel(shots, slabs, *refs)

    def wave(*refs):
        wave_kernel(shots, slabs, *refs)

    gathered, fields = pl.pallas_call(
        exchange,
        out_shape=(
            jax.ShapeDtypeStruct((slabs, shots, 2, depth, LANES), jnp.bfloat16),
            jax.ShapeDtypeStruct((slabs, 2, depth, width), jnp.float32),
        ),
        in_specs=[hbm] * 7,
        out_specs=(hbm, hbm),
        scratch_shapes=[
            pltpu.VMEM((shots, 2, depth, LANES), jnp.bfloat16),
            pltpu.VMEM((2, depth, width), jnp.float32),
            pltpu.SemaphoreType.DMA((shots,)),
            pltpu.SemaphoreType.DMA((shots,)),
            pltpu.SemaphoreType.DMA((slabs,)),
            pltpu.SemaphoreType.DMA((slabs,)),
            pltpu.SemaphoreType.DMA((slabs, shots)),
            pltpu.SemaphoreType.DMA((slabs, shots)),
            pltpu.VMEM((3 * ROWS, NS), jnp.bfloat16),
            pltpu.VMEM((depth, width), jnp.float32),
            pltpu.VMEM((depth, width), jnp.float32),
            pltpu.VMEM(velocity.shape, jnp.bfloat16),
            pltpu.VMEM((rows, NS), jnp.bfloat16),
            pltpu.VMEM((1, rows), jnp.int32),
            pltpu.VMEM((1, rows), jnp.int32),
            pltpu.SemaphoreType.DMA((7,)),
        ],
        compiler_params=pltpu.CompilerParams(
            collective_id=0, has_side_effects=True, vmem_limit_bytes=63 << 20
        ),
    )(
        split_table(), field_now, field_before, velocity, traces[0],
        trace_shot.reshape(1, rows), trace_node_cell,
    )
    return pl.pallas_call(
        wave,
        out_shape=jax.ShapeDtypeStruct((depth, width), jnp.float32),
        in_specs=[smem, smem, hbm, hbm],
        out_specs=vmem,
        scratch_shapes=[
            pltpu.VMEM((slabs, STEPS * depth, width), jnp.float32),
            pltpu.VMEM((2, STEPS * depth, shots * LANES), jnp.bfloat16),
            pltpu.VMEM((2, width, shots * LANES), jnp.bfloat16),
            pltpu.VMEM((slabs, depth, width), jnp.float32),
            pltpu.VMEM((slabs, depth, width), jnp.float32),
            pltpu.VMEM((slabs, depth, width), jnp.float32),
            pltpu.VMEM((slabs, shots, 2, depth, LANES), jnp.bfloat16),
            pltpu.SemaphoreType.DMA((3,)),
        ],
        compiler_params=pltpu.CompilerParams(vmem_limit_bytes=63 << 20),
    )(offsets, source_cell, gathered, fields)


def solution(mesh):
    in_specs = (
        P("slab", ("groups", "shot")),
        P("slab", ("groups", "shot")),
        P("slab", ("groups", "shot")),
        P(("groups", "shot")),
        P(("groups", "shot")),
        P("slab", ("groups", "shot"), None),
        P("slab", ("groups", "shot"), None),
        P("slab", ("groups", "shot")),
    )
    out_specs = P("slab", ("groups", "shot"))
    return jax.shard_map(local, mesh=mesh, in_specs=in_specs, out_specs=out_specs, check_vma=False)
```
